1024 devices in a mesh: dp: 32 (over x, z_lo), space: 8 (over z_hi, core), tm: 4 (over y).
Axes of the slice: x: 4, y: 4, z: 32 (z_hi: 4, z_lo: 8; z = z_hi * 8 + z_lo), core: 2. Of those that a mesh axis runs over, the one named last changes fastest.
Arguments:
- inputs: bfloat16 [32, 20, 128, 1024], P('dp', None, 'space', 'tm'), may hold values from -6 to 6
- out_grad: bfloat16 [32, 20, 128, 1024], P('dp', None, 'space', 'tm'), may hold values from -6 to 6
- norm_gain: float32 [1024], replicated, may hold values from 0.1 to 1.9
- pos_bias: float32 [16, 39], P('tm'), may hold values from -4 to 4
- w_query: bfloat16 [1024, 1024], P(None, 'tm'), may hold values from -0.1875 to 0.1875
- w_key: bfloat16 [1024, 1024], P(None, 'tm'), may hold values from -0.1875 to 0.1875
- w_value: bfloat16 [1024, 1024], P(None, 'tm'), may hold values from -0.1875 to 0.1875
- w_out: bfloat16 [1024, 1024], P('tm'), may hold values from -0.1875 to 0.1875
Outputs:
- block_out: bfloat16 [32, 20, 128, 1024], P('dp', None, 'space', 'tm')
- input_grad: bfloat16 [32, 20, 128, 1024], P('dp', None, 'space', 'tm')
- gain_grad: float32 [1024], P('tm')
- bias_grad: float32 [16, 39], P('tm')
The draws below stay inside these ranges and needn't reach their ends.
All inputs are finite; a program needn't handle non-finite values.
Results may differ from the reference program's by a relative error of at most 0.0099.
Values may be sent and summed in bfloat16 or wider, within the bound.
A program may use at most 32 MiB of HBM per device.

```python
import jax
import jax.numpy as jnp
from jax import lax

HEADS = 16
HEAD_DIM = 64
C = 1024
FRAMES = 20
PIXELS = 128
CLIPS = 32


def levels(stream_key, extent, pieces, low, top_value):
    loudness = 1.0
    for dim, shards_of in pieces:
        draws = jax.random.uniform(jax.random.fold_in(jax.random.fold_in(stream_key, 6), dim), (shards_of,), jnp.float32, low / len(pieces), top_value / len(pieces))
        loudness = loudness * jnp.repeat(jnp.exp(draws), extent[dim] // shards_of).reshape((-1,) + (1,) * (len(extent) - 1 - dim))
    return loudness


def bell_draw(rng, shape, spread, bound, shards=(), kind=jnp.bfloat16):
    gain = levels(rng, shape, shards, -0.22, 0.18) if shards else 1.0
    result = jax.random.normal(rng, shape, jnp.float32) * spread * gain
    return jnp.minimum(jnp.maximum(result, -bound), bound).astype(kind)


def setup_inputs(seed: int = 0) -> dict:
    seeds = jax.random.split(jax.random.key(seed), 9)
    inputs = bell_draw(seeds[0], (CLIPS, FRAMES, PIXELS, C), 1.0, 6.0, ((0, 32), (2, 8), (3, 4)))
    out_grad = bell_draw(seeds[1], (CLIPS, FRAMES, PIXELS, C), 1.0, 6.0, ((0, 32), (2, 8), (3, 4)))
    norm_gain = jnp.clip(1.0 + 0.18 * jax.random.normal(seeds[2], (C,), jnp.float32), 0.1, 1.9)
    pos_bias = bell_draw(seeds[3], (HEADS, 2 * FRAMES - 1), 1.0, 4.0, ((0, 4),), jnp.float32)
    w_query = bell_draw(seeds[4], (C, C), C ** -0.5, 0.1875, ((1, 4),))
    w_key = bell_draw(seeds[5], (C, C), C ** -0.5, 0.1875, ((1, 4),))
    w_value = bell_draw(seeds[6], (C, C), C ** -0.5, 0.1875, ((1, 4),))
    w_out = bell_draw(seeds[7], (C, C), C ** -0.5, 0.1875, ((0, 4),))
    return dict(inputs=inputs, out_grad=out_grad, norm_gain=norm_gain, pos_bias=pos_bias, w_query=w_query, w_key=w_key, w_value=w_value, w_out=w_out)


def reference(inputs, out_grad, norm_gain, pos_bias, w_query, w_key, w_value, w_out):
    frames = inputs.shape[1]
    chans = inputs.shape[3]
    scale = HEAD_DIM ** (-0.5)
    offsets = jnp.arange(frames)[None, :] - jnp.arange(frames)[:, None] + frames - 1
    rel_bias = pos_bias[:, offsets]

    def one_clip(pair):
        clip_in, clip_grad = pair
        pixels = clip_in.shape[1]
        x_full = clip_in.astype(jnp.float32)
        scale_inv = lax.rsqrt(lax.optimization_barrier(jnp.mean(x_full * x_full, axis=-1, keepdims=True)) + 1e-06)
        normed = (x_full * scale_inv * norm_gain).astype(jnp.bfloat16).reshape(-1, chans)

        def project(weight):
            out = jnp.dot(normed, weight, preferred_element_type=jnp.float32).astype(jnp.bfloat16)
            return out.reshape(frames, pixels, HEADS, HEAD_DIM).astype(jnp.float32)
        queries = project(w_query)
        key_rows = project(w_key)
        value_rows = project(w_value)
        scores = jnp.einsum('qphd,kphd->phqk', queries, key_rows) * scale + rel_bias[None]
        log_total = jax.nn.logsumexp(scores, axis=-1, keepdims=True)
        probs = jnp.exp(scores - log_total).astype(jnp.bfloat16).astype(jnp.float32)
        attended = jnp.einsum('phqk,kphd->qphd', probs, value_rows).astype(jnp.bfloat16)
        mixed = jnp.dot(attended.reshape(-1, chans), w_out, preferred_element_type=jnp.float32)
        block_out = (x_full + mixed.reshape(frames, pixels, chans)).astype(jnp.bfloat16)
        grad_att = jnp.dot(clip_grad.reshape(-1, chans), w_out.T, preferred_element_type=jnp.float32)
        grad_att = grad_att.astype(jnp.bfloat16).reshape(frames, pixels, HEADS, HEAD_DIM).astype(jnp.float32)
        grad_prob = jnp.einsum('qphd,kphd->phqk', grad_att, value_rows)
        row_dot = lax.optimization_barrier(jnp.sum(probs * grad_prob, axis=-1, keepdims=True))
        grad_score = probs * (grad_prob - row_dot)
        grad_scaled = (grad_score * scale).astype(jnp.bfloat16).astype(jnp.float32)
        grad_query = jnp.einsum('phqk,kphd->qphd', grad_scaled, key_rows).astype(jnp.bfloat16)
        grad_key = jnp.einsum('phqk,qphd->kphd', grad_scaled, queries).astype(jnp.bfloat16)
        grad_value = jnp.einsum('phqk,qphd->kphd', probs, grad_att).astype(jnp.bfloat16)
        grad_normed = jnp.dot(grad_query.reshape(-1, chans), w_query.T, preferred_element_type=jnp.float32)
        grad_normed = grad_normed + jnp.dot(grad_key.reshape(-1, chans), w_key.T, preferred_element_type=jnp.float32)
        grad_normed = grad_normed + jnp.dot(grad_value.reshape(-1, chans), w_value.T, preferred_element_type=jnp.float32)
        grad_normed = grad_normed.reshape(frames, pixels, chans)
        gain_grad = lax.optimization_barrier(jnp.sum(grad_normed * x_full * scale_inv, axis=(0, 1)))
        scaled_grad = grad_normed * norm_gain
        inner = lax.optimization_barrier(jnp.mean(scaled_grad * x_full, axis=-1, keepdims=True))
        input_grad = clip_grad.astype(jnp.float32) + scale_inv * scaled_grad - x_full * scale_inv ** 3 * inner
        score_sum = lax.optimization_barrier(jnp.sum(grad_score, axis=0))
        bias_grad = jnp.zeros((HEADS, 2 * frames - 1), jnp.float32).at[:, offsets].add(score_sum)
        return (block_out, input_grad.astype(jnp.bfloat16), gain_grad, bias_grad)
    block_out, input_grad, gain_grad, bias_grad = lax.map(one_clip, (inputs, out_grad))
    return (block_out, input_grad, lax.optimization_barrier(jnp.sum(gain_grad, axis=0)), lax.optimization_barrier(jnp.sum(bias_grad, axis=0)))
```

```python
import functools

import jax
import jax.numpy as jnp
from jax import lax
from jax.experimental import pallas as pl
from jax.experimental.pallas import tpu as pltpu
from jax.sharding import PartitionSpec as P

F32 = jnp.float32
BF16 = jnp.bfloat16
I32 = jnp.int32
NEG = -1e30
LANES = 128


def nn(a, b, precision=None):
    return lax.dot_general(
        a, b, (((1,), (0,)), ((), ())), precision=precision, preferred_element_type=F32
    )


def nt(a, b, precision=None):
    return lax.dot_general(
        a, b, (((1,), (1,)), ((), ())), precision=precision, preferred_element_type=F32
    )


def iota(shape, dim):
    return lax.broadcasted_iota(I32, shape, dim)


def onehot_rows(rows, cols, per):
    return (lax.div(iota((rows, cols), 0), per) == iota((rows, cols), 1)).astype(F32)


def onehot_cols(rows, cols, per):
    return (lax.div(iota((rows, cols), 1), per) == iota((rows, cols), 0)).astype(F32)


def kernel(
    cfg,
    x_hbm,
    g_hbm,
    gain_hbm,
    bias_hbm,
    wq_hbm,
    wk_hbm,
    wv_hbm,
    wo_hbm,
    bo_hbm,
    ig_hbm,
    gg_ref,
    bb_ref,
    x_all,
    g_all,
    w_all,
    wo,
    gain,
    bias,
    bm,
    probs,
    xg,
    qm,
    km,
    vm,
    gam,
    ks,
    vs,
    q_t,
    ga_t,
    sinv,
    att,
    gq_acc,
    gk_t,
    gv_t,
    gcat,
    gsum,
    mix_own,
    mix_send,
    mix_recv,
    ig_own,
    ig_send,
    ig_recv,
    p0_send,
    p0_recv,
    pay1,
    near_recv,
    pay2,
    far_recv,
    bo_st,
    ig_st,
    lsem,
    xsend,
    xrecv,
    gsend,
    grecv,
    msend,
    mrecv,
    isend,
    irecv,
    p0s,
    p0r,
    nsend,
    nrecv,
    fsend,
    frecv,
):
    frames, pixels, heads, n, xs, zl, zh, cores = cfg
    rows, width = x_hbm.shape
    chans = width * n
    head_dim = width // heads
    scale = head_dim ** (-0.5)
    me = lax.axis_index("tm")
    dp = lax.axis_index("dp")
    sp = lax.axis_index("space")
    my_x, my_zl = lax.div(dp, zl), lax.rem(dp, zl)
    my_zh, my_core = lax.div(sp, cores), lax.rem(sp, cores)

    ring = [(dp, sp, lax.rem(me + a, n)) for a in range(n)]
    shard = [lax.rem(me + a, n) for a in range(n)]
    near = [
        (my_x * zl + lax.rem(my_zl + b, zl), my_zh * cores + lax.rem(my_core + d, cores), me)
        for b in range(zl)
        for d in range(cores)
        if b or d
    ]
    far = [
        (lax.rem(my_x + b, xs) * zl + my_zl, lax.rem(my_zh + d, zh) * cores + my_core, me)
        for b in range(xs)
        for d in range(zh)
        if b or d
    ]

    def send(src, dst, ssem, rsem, to):
        return pltpu.make_async_remote_copy(
            src_ref=src,
            dst_ref=dst,
            send_sem=ssem,
            recv_sem=rsem,
            device_id=to,
            device_id_type=pl.DeviceIdType.MESH,
        )

    def cols(a):
        return pl.ds(pl.multiple_of(shard[a] * width, width), width)

    loads = [
        pltpu.make_async_copy(x_hbm, x_all.at[me], lsem.at[0]),
        pltpu.make_async_copy(gain_hbm, gain, lsem.at[1]),
        pltpu.make_async_copy(bias_hbm, bias, lsem.at[2]),
        pltpu.make_async_copy(wq_hbm, w_all.at[:, pl.ds(0, width)], lsem.at[3]),
        pltpu.make_async_copy(wk_hbm, w_all.at[:, pl.ds(width, width)], lsem.at[4]),
        pltpu.make_async_copy(wv_hbm, w_all.at[:, pl.ds(2 * width, width)], lsem.at[5]),
        pltpu.make_async_copy(wo_hbm, wo, lsem.at[6]),
        pltpu.make_async_copy(g_hbm, g_all.at[me], lsem.at[7]),
    ]
    for load in loads:
        load.start()

    barrier = pltpu.get_barrier_semaphore()
    peers = ring[1:] + near + far
    for peer in peers:
        pl.semaphore_signal(
            barrier, inc=1, device_id=peer, device_id_type=pl.DeviceIdType.MESH
        )
    pl.semaphore_wait(barrier, len(peers))

    order = [2, 1, 3] if n == 4 else list(range(1, n))
    x_out = [
        send(x_hbm, x_all.at[me], xsend.at[a - 1], xrecv.at[a - 1], ring[a])
        for a in range(1, n)
    ]
    g_out = [
        send(g_hbm, g_all.at[me], gsend.at[a - 1], grecv.at[a - 1], ring[a])
        for a in range(1, n)
    ]
    for a in order:
        x_out[a - 1].start()

    loads[2].wait()
    by_row = onehot_rows(rows, 32, pixels)
    by_col = onehot_cols(LANES, rows, pixels)
    same = lax.rem(iota((rows, rows), 0), pixels) == lax.rem(iota((rows, rows), 1), pixels)
    offs = 2 * frames - 1
    ahead = lax.rem(iota((offs, LANES), 1) + (frames - 1), LANES)
    spread = (iota((offs, LANES), 0) == ahead).astype(F32)
    wide = nn(bias[...], spread, lax.Precision.HIGHEST)
    for h in range(heads):
        line = jnp.broadcast_to(wide[h : h + 1, :], (32, LANES))
        table = pltpu.roll(line, 0, 1, stride=1, stride_axis=0)
        tall = nn(by_row, table, lax.Precision.HIGHEST)
        full = nn(tall, by_col, lax.Precision.HIGHEST)
        bm[h] = jnp.where(same, full, NEG)

    for load in loads[:2] + loads[3:]:
        load.wait()

    square = jnp.zeros((rows, 1), F32)
    for a in [0] + [n - b for b in order[1:] + order[:1]]:
        if a:
            x_out[n - a - 1].wait_recv()
        part = x_all[shard[a]].astype(F32)
        square = square + jnp.sum(part * part, axis=1, keepdims=True)
        xg[:, cols(a)] = (part * gain[:, cols(a)]).astype(BF16)
    for a in order:
        x_out[a - 1].wait_send()
    for a in order:
        g_out[a - 1].start()
    inv = lax.rsqrt(square * (1.0 / chans) + 1e-06)
    sinv[...] = jnp.broadcast_to(inv, (rows, LANES))

    head_of = lax.div(iota((rows, width), 1), head_dim)
    eye = (iota((width, width), 0) == iota((width, width), 1)).astype(BF16)

    qkv = nn(xg[...], w_all[...]) * inv
    q = (qkv[:, :width].astype(BF16).astype(F32) * scale).astype(BF16)
    k = qkv[:, width : 2 * width].astype(BF16)
    v = qkv[:, 2 * width :].astype(BF16)
    ks[...] = k
    vs[...] = v
    q_t[...] = nt(eye, q).astype(BF16)
    for h in range(heads):
        qm[h] = jnp.where(head_of == h, q.astype(F32), 0.0).astype(BF16)
        km[h] = jnp.where(head_of == h, k.astype(F32), 0.0).astype(BF16)
        vm[h] = jnp.where(head_of == h, v.astype(F32), 0.0).astype(BF16)

    att[...] = jnp.zeros((rows, width), F32)
    for h in range(heads):
        scores = nt(qm[h], ks[...]) + bm[h]
        top = jnp.max(scores, axis=1, keepdims=True)
        e = jnp.exp(scores - top)
        total = jnp.sum(e, axis=1, keepdims=True)
        p = (e * (1.0 / total)).astype(BF16)
        probs[h] = p
        att[...] += nn(p, vm[h])

    att_b = att[...].astype(BF16)
    m_out = [
        send(mix_send.at[a - 1], mix_recv.at[a - 1], msend.at[a - 1], mrecv.at[a - 1], ring[a])
        for a in range(1, n)
    ]
    for a in order:
        mix_send[a - 1] = nn(att_b, wo[:, cols(a)]).astype(BF16)
        m_out[a - 1].start()
    mix_own[...] = nn(att_b, wo[:, cols(0)])

    for a in range(1, n):
        g_out[a - 1].wait()
    ga_f = nt(g_all[0], wo[:, :width])
    for s in range(1, n):
        ga_f = ga_f + nt(g_all[s], wo[:, s * width : (s + 1) * width])
    ga = ga_f.astype(BF16)
    ga_t[...] = nt(eye, ga).astype(BF16)
    for h in range(heads):
        gam[h] = jnp.where(head_of == h, ga.astype(F32), 0.0).astype(BF16)

    last_first = (
        lax.div(iota((32, rows), 1), pixels) == (frames - 1) - iota((32, rows), 0)
    ).astype(BF16)
    gq_acc[...] = jnp.zeros((rows, width), F32)
    for h in range(heads):
        at = pl.ds(h * head_dim, head_dim)
        p = probs[h].astype(F32)
        grad_p = nt(gam[h], vs[...])
        dot = jnp.sum(p * grad_p, axis=1, keepdims=True)
        grad_s = (p * (grad_p - dot)).astype(BF16)
        gq_acc[...] += nn(grad_s, km[h])
        gk_t[at, :] = nn(q_t[at, :], grad_s).astype(BF16)
        gv_t[at, :] = nn(ga_t[at, :], probs[h]).astype(BF16)
        gsum[h] = nn(last_first, grad_s)

    eye_r = (iota((rows, rows), 0) == iota((rows, rows), 1)).astype(BF16)
    gq = (gq_acc[...] * scale).astype(BF16)
    gk_f = nt(eye_r, gk_t[...])
    gv_f = nt(eye_r, gv_t[...])
    gcat[:, :width] = gq
    gcat[:, width : 2 * width] = gk_f.astype(BF16)
    gcat[:, 2 * width :] = gv_f.astype(BF16)
    qf = functools.reduce(jnp.add, [qm[h] for h in range(heads)])
    dots = (
        gq.astype(F32) * qf.astype(F32) * (1.0 / scale)
        + gk_f * ks[...].astype(F32)
        + gv_f * vs[...].astype(F32)
    )
    inv = sinv[:, :1]
    mean = jnp.sum(dots, axis=1, keepdims=True) * (inv * inv * (1.0 / chans))

    i_out = [
        send(ig_send.at[a - 1], ig_recv.at[a - 1], isend.at[a - 1], irecv.at[a - 1], ring[a])
        for a in range(1, n)
    ]
    p_out = [
        send(p0_send.at[a - 1], p0_recv.at[a - 1], p0s.at[a - 1], p0r.at[a - 1], ring[a])
        for a in range(1, n)
    ]
    own_gain = None
    for a in order + [0]:
        back = nt(gcat[...], w_all[cols(a), :])
        part = x_all[shard[a]].astype(F32)
        gain_part = jnp.sum(back * (part * inv), axis=0, keepdims=True)
        share = back * (gain[:, cols(a)] * inv) - part * mean
        if a:
            p0_send[a - 1] = gain_part
            p_out[a - 1].start()
            ig_send[a - 1] = share.astype(BF16)
            i_out[a - 1].start()
        else:
            own_gain = gain_part
            ig_own[...] = share

    by_key = onehot_rows(rows, LANES, pixels)
    for h in range(heads):
        pairs = nn(gsum[h], by_key, lax.Precision.HIGHEST)
        moved = pltpu.roll(pairs, 0, 1, stride=1, stride_axis=0)
        pay1[:, width + LANES * h : width + LANES * (h + 1)] = jnp.sum(moved, axis=0, keepdims=True)

    for a in range(1, n):
        p_out[a - 1].wait()
        own_gain = own_gain + p0_recv[a - 1]
    pay1[:, :width] = own_gain
    n_out = [
        send(pay1, near_recv.at[j], nsend.at[j], nrecv.at[j], peer) for j, peer in enumerate(near)
    ]
    for copy in n_out:
        copy.start()

    for a in range(1, n):
        m_out[a - 1].wait()
    mixed = mix_own[...]
    for a in range(1, n):
        mixed = mixed + mix_recv[a - 1].astype(F32)
    bo_st[...] = (x_all[me].astype(F32) + mixed).astype(BF16)
    store_bo = pltpu.make_async_copy(bo_st, bo_hbm, lsem.at[8])
    store_bo.start()

    total = pay1[...]
    for j, copy in enumerate(n_out):
        copy.wait()
        total = total + near_recv[j]
    pay2[...] = total
    f_out = [
        send(pay2, far_recv.at[j], fsend.at[j], frecv.at[j], peer) for j, peer in enumerate(far)
    ]
    for copy in f_out:
        copy.start()

    for a in range(1, n):
        i_out[a - 1].wait()
    grad = ig_own[...] + g_all[me].astype(F32)
    for a in range(1, n):
        grad = grad + ig_recv[a - 1].astype(F32)
    ig_st[...] = grad.astype(BF16)
    store_ig = pltpu.make_async_copy(ig_st, ig_hbm, lsem.at[9])
    store_ig.start()

    total = pay2[...]
    for j, copy in enumerate(f_out):
        copy.wait()
        total = total + far_recv[j]
    gg_ref[...] = total[:, :width]
    for h in range(heads):
        bb_ref[h : h + 1, :] = total[:, width + LANES * h : width + LANES * h + offs]
    store_bo.wait()
    store_ig.wait()


def split_axis(size, parts):
    return (size // parts, parts) if size % parts == 0 else (size, 1)


def per_device(mesh_shape, inputs, out_grad, norm_gain, pos_bias, w_query, w_key, w_value, w_out):
    clips, frames, pixels, width = inputs.shape
    heads = pos_bias.shape[0]
    n = mesh_shape["tm"]
    chans = width * n
    rows = clips * frames * pixels
    xs, zl = split_axis(mesh_shape["dp"], 8)
    zh, cores = split_axis(mesh_shape["space"], 2)
    near, far = zl * cores - 1, xs * zh - 1
    pay = width + LANES * heads
    cfg = (frames, pixels, heads, n, xs, zl, zh, cores)
    vmem, dma = pltpu.VMEM, pltpu.SemaphoreType.DMA
    anywhere = pl.BlockSpec(memory_space=pl.ANY)
    in_vmem = pl.BlockSpec(memory_space=pltpu.VMEM)
    bo, ig, gg, bb = pl.pallas_call(
        functools.partial(kernel, cfg),
        out_shape=(
            jax.ShapeDtypeStruct((rows, width), BF16),
            jax.ShapeDtypeStruct((rows, width), BF16),
            jax.ShapeDtypeStruct((1, width), F32),
            jax.ShapeDtypeStruct(pos_bias.shape, F32),
        ),
        in_specs=[anywhere] * 8,
        out_specs=(anywhere, anywhere, in_vmem, in_vmem),
        scratch_shapes=[
            vmem((n, rows, width), BF16),
            vmem((n, rows, width), BF16),
            vmem((chans, 3 * width), BF16),
            vmem((width, chans), BF16),
            vmem((1, chans), F32),
            vmem(pos_bias.shape, F32),
            vmem((heads, rows, rows), F32),
            vmem((heads, rows, rows), BF16),
            vmem((rows, chans), BF16),
            vmem((heads, rows, width), BF16),
            vmem((heads, rows, width), BF16),
            vmem((heads, rows, width), BF16),
            vmem((heads, rows, width), BF16),
            vmem((rows, width), BF16),
            vmem((rows, width), BF16),
            vmem((width, rows), BF16),
            vmem((width, rows), BF16),
            vmem((rows, LANES), F32),
            vmem((rows, width), F32),
            vmem((rows, width), F32),
            vmem((width, rows), BF16),
            vmem((width, rows), BF16),
            vmem((rows, 3 * width), BF16),
            vmem((heads, 32, rows), F32),
            vmem((rows, width), F32),
            vmem((n - 1, rows, width), BF16),
            vmem((n - 1, rows, width), BF16),
            vmem((rows, width), F32),
            vmem((n - 1, rows, width), BF16),
            vmem((n - 1, rows, width), BF16),
            vmem((n - 1, 1, width), F32),
            vmem((n - 1, 1, width), F32),
            vmem((1, pay), F32),
            vmem((near, 1, pay), F32),
            vmem((1, pay), F32),
            vmem((far, 1, pay), F32),
            vmem((rows, width), BF16),
            vmem((rows, width), BF16),
            dma((10,)),
        ]
        + [dma((n - 1,))] * 10
        + [dma((near,)), dma((near,)), dma((far,)), dma((far,))],
        compiler_params=pltpu.CompilerParams(
            collective_id=0, has_side_effects=True, vmem_limit_bytes=56 * 1024 * 1024
        ),
    )(
        inputs.reshape(rows, width),
        out_grad.reshape(rows, width),
        norm_gain.reshape(1, chans),
        pos_bias,
        w_query,
        w_key,
        w_value,
        w_out,
    )
    return bo.reshape(inputs.shape), ig.reshape(inputs.shape), gg.reshape(width), bb


def solution(mesh):
    return jax.shard_map(
        functools.partial(per_device, dict(mesh.shape)),
        mesh=mesh,
        in_specs=(
            P("dp", None, "space", "tm"),
            P("dp", None, "space", "tm"),
            P(),
            P("tm", None),
            P(None, "tm"),
            P(None, "tm"),
            P(None, "tm"),
            P("tm", None),
        ),
        out_specs=(
            P("dp", None, "space", "tm"),
            P("dp", None, "space", "tm"),
            P("tm"),
            P("tm", None),
        ),
        check_vma=False,
    )
```

```python
import functools

import jax
import jax.numpy as jnp
from jax import lax
from jax.experimental import pallas as pl
from jax.experimental.pallas import tpu as pltpu
from jax.sharding import PartitionSpec as P

F32 = jnp.float32
BF16 = jnp.bfloat16
I32 = jnp.int32
NEG = -1e30
LANES = 128


def nn(a, b, precision=None):
    return lax.dot_general(
        a, b, (((1,), (0,)), ((), ())), precision=precision, preferred_element_type=F32
    )


def nt(a, b, precision=None):
    return lax.dot_general(
        a, b, (((1,), (1,)), ((), ())), precision=precision, preferred_element_type=F32
    )


def iota(shape, dim):
    return lax.broadcasted_iota(I32, shape, dim)


def onehot_rows(rows, cols, per):
    return (lax.div(iota((rows, cols), 0), per) == iota((rows, cols), 1)).astype(F32)


def onehot_cols(rows, cols, per):
    return (lax.div(iota((rows, cols), 1), per) == iota((rows, cols), 0)).astype(F32)


def kernel(
    cfg,
    x_hbm,
    g_hbm,
    gain_hbm,
    bias_hbm,
    wq_hbm,
    wk_hbm,
    wv_hbm,
    wo_hbm,
    bo_hbm,
    ig_hbm,
    gg_ref,
    bb_ref,
    x_all,
    g_all,
    w_all,
    wo,
    gain,
    bias,
    bm,
    probs,
    xg,
    qm,
    km,
    vm,
    gam,
    ks,
    vs,
    q_t,
    ga_t,
    sinv,
    att,
    gq_acc,
    gk_t,
    gv_t,
    gcat,
    gsum,
    mix_own,
    mix_opp,
    mix_dir,
    mix_part,
    mix_sum,
    mix_ropp,
    mix_rdir,
    mix_rsum,
    ig_own,
    ig_opp,
    ig_dir,
    ig_part,
    ig_sum,
    ig_ropp,
    ig_rdir,
    ig_rsum,
    slices,
    slices_recv,
    pay0,
    pay0_recv,
    pay1,
    mid_recv,
    pay2,
    far_recv,
    bo_st,
    ig_st,
    lsem,
    xsend,
    xrecv,
    gsend,
    grecv,
    msend,
    mrecv,
    isend,
    irecv,
    ssend,
    srecv,
    csend,
    crecv,
    nsend,
    nrecv,
    fsend,
    frecv,
):
    frames, pixels, heads, n, xs, za_lo, za_hi, zb, cores = cfg
    rows, width = x_hbm.shape
    chans = width * n
    head_dim = width // heads
    scale = head_dim ** (-0.5)
    half = rows // 2
    lo, hi = pl.ds(0, half), pl.ds(half, half)
    me = lax.axis_index("tm")
    dp = lax.axis_index("dp")
    sp = lax.axis_index("space")
    my_core = lax.rem(sp, cores)
    run = lax.rem(dp, za_lo * zb)
    my_x, my_zb = lax.div(dp, za_lo * zb), lax.rem(run, zb)
    my_za = lax.div(sp, cores) * za_lo + lax.div(run, zb)

    def device(x, a, b, core, y):
        return (
            (x * za_lo + lax.rem(a, za_lo)) * zb + b,
            lax.div(a, za_lo) * cores + core,
            y,
        )

    shard = [lax.rem(me + a, n) for a in range(n)]
    ring = [(dp, sp, shard[a]) for a in range(n)]
    slice_to = [
        (a, device(my_x, my_za, my_zb, lax.rem(my_core + c, cores), shard[a]))
        for a in (2, 1, 3)
        for c in range(cores)
    ]
    twins = [
        device(my_x, my_za, my_zb, lax.rem(my_core + c, cores), me) for c in range(1, cores)
    ]
    mid = [
        device(lax.rem(my_x + b, xs), my_za, lax.rem(my_zb + d, zb), my_core, me)
        for b in range(xs)
        for d in range(zb)
        if b or d
    ]
    far = [
        device(my_x, lax.rem(my_za + a, za_lo * za_hi), my_zb, my_core, me)
        for a in range(1, za_lo * za_hi)
    ]

    def send(src, dst, ssem, rsem, to):
        return pltpu.make_async_remote_copy(
            src_ref=src,
            dst_ref=dst,
            send_sem=ssem,
            recv_sem=rsem,
            device_id=to,
            device_id_type=pl.DeviceIdType.MESH,
        )

    def gather(src, dst, ssem, rsem):
        moves = [
            (src.at[lo], dst.at[me, lo], 1),
            (src.at[hi], dst.at[me, hi], 3),
            (src.at[hi], dst.at[me, hi], 1),
            (src.at[lo], dst.at[me, lo], 3),
            (dst.at[shard[3], lo], dst.at[shard[3], lo], 1),
            (dst.at[shard[1], hi], dst.at[shard[1], hi], 3),
        ]
        return [
            send(s, d, ssem.at[i], rsem.at[i], ring[a]) for i, (s, d, a) in enumerate(moves)
        ]

    def scatter(opp, direct, total, ropp, rdir, rsum, ssem, rsem):
        moves = [
            (opp.at[lo], ropp.at[0], 1),
            (opp.at[hi], ropp.at[1], 3),
            (direct.at[0], rdir.at[0], 3),
            (direct.at[1], rdir.at[1], 1),
            (total.at[0], rsum.at[0], 1),
            (total.at[1], rsum.at[1], 3),
        ]
        return [
            send(s, d, ssem.at[i], rsem.at[i], ring[a]) for i, (s, d, a) in enumerate(moves)
        ]

    def cols(a):
        return pl.ds(pl.multiple_of(shard[a] * width, width), width)

    loads = [
        pltpu.make_async_copy(bias_hbm, bias, lsem.at[2]),
        pltpu.make_async_copy(x_hbm, x_all.at[me], lsem.at[0]),
        pltpu.make_async_copy(gain_hbm, gain, lsem.at[1]),
        pltpu.make_async_copy(wq_hbm, w_all.at[:, pl.ds(0, width)], lsem.at[3]),
        pltpu.make_async_copy(wk_hbm, w_all.at[:, pl.ds(width, width)], lsem.at[4]),
        pltpu.make_async_copy(wv_hbm, w_all.at[:, pl.ds(2 * width, width)], lsem.at[5]),
        pltpu.make_async_copy(wo_hbm, wo, lsem.at[6]),
        pltpu.make_async_copy(g_hbm, g_all.at[me], lsem.at[7]),
    ]
    for load in loads:
        load.start()

    barrier = pltpu.get_barrier_semaphore()
    peers = [to for _, to in slice_to] + twins + mid + far
    for peer in peers:
        pl.semaphore_signal(
            barrier, inc=1, device_id=peer, device_id_type=pl.DeviceIdType.MESH
        )

    loads[0].wait()
    by_row = onehot_rows(rows, 32, pixels)
    by_col = onehot_cols(LANES, rows, pixels)
    same = lax.rem(iota((rows, rows), 0), pixels) == lax.rem(iota((rows, rows), 1), pixels)
    offs = 2 * frames - 1
    ahead = lax.rem(iota((offs, LANES), 1) + (frames - 1), LANES)
    spread = (iota((offs, LANES), 0) == ahead).astype(F32)
    wide = nn(bias[...], spread, lax.Precision.HIGHEST)
    for h in range(heads):
        line = jnp.broadcast_to(wide[h : h + 1, :], (32, LANES))
        table = pltpu.roll(line, 0, 1, stride=1, stride_axis=0)
        tall = nn(by_row, table, lax.Precision.HIGHEST)
        full = nn(tall, by_col, lax.Precision.HIGHEST)
        bm[h] = jnp.where(same, full, NEG)

    pl.semaphore_wait(barrier, len(peers))

    x_out = gather(x_hbm, x_all, xsend, xrecv)
    g_out = gather(g_hbm, g_all, gsend, grecv)
    for copy in x_out[:4]:
        copy.start()
    for load in loads[1:]:
        load.wait()

    def take(a, square):
        part = x_all[shard[a]].astype(F32)
        xg[:, cols(a)] = (part * gain[:, cols(a)]).astype(BF16)
        return square + jnp.sum(part * part, axis=1, keepdims=True)

    square = take(0, jnp.zeros((rows, 1), F32))
    x_out[0].wait_recv()
    x_out[4].start()
    x_out[1].wait_recv()
    x_out[5].start()
    for copy in g_out[:4]:
        copy.start()
    x_out[2].wait_recv()
    square = take(3, square)
    x_out[3].wait_recv()
    square = take(1, square)
    x_out[4].wait_recv()
    x_out[5].wait_recv()
    square = take(2, square)
    inv = lax.rsqrt(square * (1.0 / chans) + 1e-06)
    sinv[...] = jnp.broadcast_to(inv, (rows, LANES))

    head_of = lax.div(iota((rows, width), 1), head_dim)
    eye = (iota((width, width), 0) == iota((width, width), 1)).astype(BF16)

    qkv = nn(xg[...], w_all[...]) * inv
    q = (qkv[:, :width].astype(BF16).astype(F32) * scale).astype(BF16)
    k = qkv[:, width : 2 * width].astype(BF16)
    v = qkv[:, 2 * width :].astype(BF16)
    ks[...] = k
    vs[...] = v
    q_t[...] = nt(eye, q).astype(BF16)
    for h in range(heads):
        qm[h] = jnp.where(head_of == h, q.astype(F32), 0.0).astype(BF16)
        km[h] = jnp.where(head_of == h, k.astype(F32), 0.0).astype(BF16)
        vm[h] = jnp.where(head_of == h, v.astype(F32), 0.0).astype(BF16)

    att[...] = jnp.zeros((rows, width), F32)
    for h in range(heads):
        scores = nt(qm[h], ks[...]) + bm[h]
        top = jnp.max(scores, axis=1, keepdims=True)
        e = jnp.exp(scores - top)
        total = jnp.sum(e, axis=1, keepdims=True)
        p = (e * (1.0 / total)).astype(BF16)
        probs[h] = p
        att[...] += nn(p, vm[h])
        if h == 0:
            g_out[0].wait_recv()
            g_out[4].start()
            g_out[1].wait_recv()
            g_out[5].start()

    att_b = att[...].astype(BF16)
    m_out = scatter(mix_opp, mix_dir, mix_sum, mix_ropp, mix_rdir, mix_rsum, msend, mrecv)
    mix_opp[...] = nn(att_b, wo[:, cols(2)]).astype(BF16)
    m_out[0].start()
    m_out[1].start()
    part = nn(att_b, wo[:, cols(3)])
    mix_dir[0] = part[:half].astype(BF16)
    mix_part[1] = part[half:]
    m_out[2].start()
    part = nn(att_b, wo[:, cols(1)])
    mix_part[0] = part[:half]
    mix_dir[1] = part[half:].astype(BF16)
    m_out[3].start()
    mix_own[...] = nn(att_b, wo[:, cols(0)])

    ga_f = nt(g_all[me], wo[:, cols(0)])
    g_out[2].wait_recv()
    ga_f = ga_f + nt(g_all[shard[3]], wo[:, cols(3)])
    g_out[3].wait_recv()
    ga_f = ga_f + nt(g_all[shard[1]], wo[:, cols(1)])
    g_out[4].wait_recv()
    g_out[5].wait_recv()
    ga_f = ga_f + nt(g_all[shard[2]], wo[:, cols(2)])
    ga = ga_f.astype(BF16)
    ga_t[...] = nt(eye, ga).astype(BF16)
    for h in range(heads):
        gam[h] = jnp.where(head_of == h, ga.astype(F32), 0.0).astype(BF16)

    last_first = (
        lax.div(iota((32, rows), 1), pixels) == (frames - 1) - iota((32, rows), 0)
    ).astype(BF16)
    gq_acc[...] = jnp.zeros((rows, width), F32)
    for h in range(heads):
        at = pl.ds(h * head_dim, head_dim)
        p = probs[h].astype(F32)
        grad_p = nt(gam[h], vs[...])
        dot = jnp.sum(p * grad_p, axis=1, keepdims=True)
        grad_s = (p * (grad_p - dot)).astype(BF16)
        gq_acc[...] += nn(grad_s, km[h])
        gk_t[at, :] = nn(q_t[at, :], grad_s).astype(BF16)
        gv_t[at, :] = nn(ga_t[at, :], probs[h]).astype(BF16)
        gsum[h] = nn(last_first, grad_s)

    eye_r = (iota((rows, rows), 0) == iota((rows, rows), 1)).astype(BF16)
    gq = (gq_acc[...] * scale).astype(BF16)
    gk_f = nt(eye_r, gk_t[...])
    gv_f = nt(eye_r, gv_t[...])
    gcat[:, :width] = gq
    gcat[:, width : 2 * width] = gk_f.astype(BF16)
    gcat[:, 2 * width :] = gv_f.astype(BF16)
    qf = functools.reduce(jnp.add, [qm[h] for h in range(heads)])
    dots = (
        gq.astype(F32) * qf.astype(F32) * (1.0 / scale)
        + gk_f * ks[...].astype(F32)
        + gv_f * vs[...].astype(F32)
    )
    inv = sinv[:, :1]
    mean = jnp.sum(dots, axis=1, keepdims=True) * (inv * inv * (1.0 / chans))

    s_out = [
        send(slices.at[a - 1], slices_recv.at[j], ssend.at[j], srecv.at[j], to)
        for j, (a, to) in enumerate(slice_to)
    ]
    own_gain = None
    i_out = scatter(ig_opp, ig_dir, ig_sum, ig_ropp, ig_rdir, ig_rsum, isend, irecv)
    for a in (2, 1, 3, 0):
        back = nt(gcat[...], w_all[cols(a), :])
        part = x_all[shard[a]].astype(F32)
        gain_part = jnp.sum(back * (part * inv), axis=0, keepdims=True)
        share = back * (gain[:, cols(a)] * inv) - part * mean
        if a:
            slices[a - 1] = gain_part
            for j, (b, _) in enumerate(slice_to):
                if a == b:
                    s_out[j].start()
        if a == 0:
            own_gain = gain_part
            ig_own[...] = share
        elif a == 2:
            ig_opp[...] = share.astype(BF16)
        elif a == 1:
            ig_part[0] = share[:half]
            ig_dir[1] = share[half:].astype(BF16)
        else:
            ig_dir[0] = share[:half].astype(BF16)
            ig_part[1] = share[half:]

    by_key = onehot_rows(rows, LANES, pixels)
    for h in range(0, heads, 2):
        pair = jnp.zeros((1, LANES), F32)
        for side in range(2):
            pairs = nn(gsum[h + side], by_key, lax.Precision.HIGHEST)
            moved = pltpu.roll(pairs, 0, 1, stride=1, stride_axis=0)
            line = jnp.sum(moved, axis=0, keepdims=True)
            pair = pair + (pltpu.roll(line, LANES // 2, 1) if side else line)
        pay0[:, width + LANES // 2 * h : width + LANES // 2 * (h + 2)] = pair
    pay0[:, :width] = own_gain
    c_out = [
        send(pay0, pay0_recv.at[j], csend.at[j], crecv.at[j], to) for j, to in enumerate(twins)
    ]
    for copy in c_out:
        copy.start()

    def add_opposite(out, part, ropp, total):
        for side in range(2):
            out[side].wait_recv()
            total[side] = (part[side] + ropp[side].astype(F32)).astype(BF16)
            out[4 + side].start()

    add_opposite(m_out, mix_part, mix_ropp, mix_sum)
    for copy in i_out[:4]:
        copy.start()

    total = pay0[...]
    for j, copy in enumerate(c_out):
        copy.wait_recv()
        total = total + pay0_recv[j]
    pay1[...] = total
    for j, copy in enumerate(s_out):
        copy.wait_recv()
        pay1[:, :width] += slices_recv[j]
    n_out = [
        send(pay1, mid_recv.at[j], nsend.at[j], nrecv.at[j], peer) for j, peer in enumerate(mid)
    ]
    for copy in n_out:
        copy.start()

    def finish(first, own, out, rdir, rsum, staged):
        for copy in out[2:]:
            copy.wait_recv()
        for side in range(2):
            at = pl.ds(side * half, half)
            got = rdir[side].astype(F32) + rsum[side].astype(F32)
            staged[at, :] = (first[me, at].astype(F32) + own[at, :] + got).astype(BF16)

    add_opposite(i_out, ig_part, ig_ropp, ig_sum)
    total = pay1[...]
    for j, copy in enumerate(n_out):
        copy.wait_recv()
        total = total + mid_recv[j]
    pay2[...] = total
    f_out = [
        send(pay2, far_recv.at[j], fsend.at[j], frecv.at[j], peer) for j, peer in enumerate(far)
    ]
    for copy in f_out:
        copy.start()

    finish(x_all, mix_own, m_out, mix_rdir, mix_rsum, bo_st)
    store_bo = pltpu.make_async_copy(bo_st, bo_hbm, lsem.at[8])
    store_bo.start()
    finish(g_all, ig_own, i_out, ig_rdir, ig_rsum, ig_st)
    store_ig = pltpu.make_async_copy(ig_st, ig_hbm, lsem.at[9])
    store_ig.start()
    for copy in x_out + g_out + m_out + i_out + s_out + c_out + n_out:
        copy.wait_send()
    store_bo.wait()
    store_ig.wait()

    total = pay2[...]
    for j, copy in enumerate(f_out):
        copy.wait_recv()
        total = total + far_recv[j]
    gg_ref[...] = total[:, :width]
    for h in range(heads):
        first = width + LANES // 2 * h
        bb_ref[h : h + 1, :] = total[:, first : first + offs]
    for copy in f_out:
        copy.wait_send()


def hand_over(*refs):
    count = (len(refs) - 1) // 2
    copies = [
        pltpu.make_async_copy(src, dst, refs[-1].at[i])
        for i, (src, dst) in enumerate(zip(refs[:count], refs[count:-1]))
    ]
    for copy in copies:
        copy.start()
    for copy in copies:
        copy.wait()


def per_device(mesh_shape, inputs, out_grad, norm_gain, pos_bias, w_query, w_key, w_value, w_out):
    clips, frames, pixels, width = inputs.shape
    heads = pos_bias.shape[0]
    n = mesh_shape["tm"]
    chans = width * n
    rows = clips * frames * pixels
    half = rows // 2
    cores, zb = 2, 4 if mesh_shape["dp"] % 8 == 0 else 1
    za_lo = 2 if mesh_shape["dp"] % 8 == 0 else 1
    xs, za_hi = mesh_shape["dp"] // (za_lo * zb), mesh_shape["space"] // cores
    mid, far = max(1, xs * zb - 1), max(1, za_lo * za_hi - 1)
    pay = width + LANES // 2 * heads
    cfg = (frames, pixels, heads, n, xs, za_lo, za_hi, zb, cores)
    vmem, dma = pltpu.VMEM, pltpu.SemaphoreType.DMA
    anywhere = pl.BlockSpec(memory_space=pl.ANY)
    in_vmem = pl.BlockSpec(memory_space=pltpu.VMEM)
    sums = [
        vmem((rows, width), F32),
        vmem((rows, width), BF16),
        vmem((2, half, width), BF16),
        vmem((2, half, width), F32),
    ] + [vmem((2, half, width), BF16)] * 4
    results = (
        jax.ShapeDtypeStruct((rows, width), BF16),
        jax.ShapeDtypeStruct((rows, width), BF16),
        jax.ShapeDtypeStruct((1, width), F32),
        jax.ShapeDtypeStruct(pos_bias.shape, F32),
    )
    made = pl.pallas_call(
        functools.partial(kernel, cfg),
        out_shape=results,
        in_specs=[anywhere] * 8,
        out_specs=(anywhere, anywhere, in_vmem, in_vmem),
        scratch_shapes=[
            vmem((n, rows, width), BF16),
            vmem((n, rows, width), BF16),
            vmem((chans, 3 * width), BF16),
            vmem((width, chans), BF16),
            vmem((1, chans), F32),
            vmem(pos_bias.shape, F32),
            vmem((heads, rows, rows), F32),
            vmem((heads, rows, rows), BF16),
            vmem((rows, chans), BF16),
            vmem((heads, rows, width), BF16),
            vmem((heads, rows, width), BF16),
            vmem((heads, rows, width), BF16),
            vmem((heads, rows, width), BF16),
            vmem((rows, width), BF16),
            vmem((rows, width), BF16),
            vmem((width, rows), BF16),
            vmem((width, rows), BF16),
            vmem((rows, LANES), F32),
            vmem((rows, width), F32),
            vmem((rows, width), F32),
            vmem((width, rows), BF16),
            vmem((width, rows), BF16),
            vmem((rows, 3 * width), BF16),
            vmem((heads, 32, rows), F32),
        ]
        + sums
        + sums
        + [
            vmem((n - 1, 1, width), F32),
            vmem(((n - 1) * cores, 1, width), F32),
            vmem((1, pay), F32),
            vmem((cores - 1, 1, pay), F32),
            vmem((1, pay), F32),
            vmem((mid, 1, pay), F32),
            vmem((1, pay), F32),
            vmem((far, 1, pay), F32),
            vmem((rows, width), BF16),
            vmem((rows, width), BF16),
            dma((10,)),
        ]
        + [dma((6,))] * 8
        + [dma(((n - 1) * cores,))] * 2
        + [dma((cores - 1,))] * 2
        + [dma((mid,))] * 2
        + [dma((far,))] * 2,
        compiler_params=pltpu.CompilerParams(
            collective_id=0, has_side_effects=True, vmem_limit_bytes=56 * 1024 * 1024
        ),
    )(
        inputs.reshape(rows, width),
        out_grad.reshape(rows, width),
        norm_gain.reshape(1, chans),
        pos_bias,
        w_query,
        w_key,
        w_value,
        w_out,
    )
    bo, ig, gg, bb = pl.pallas_call(
        hand_over,
        out_shape=results,
        in_specs=[anywhere] * 4,
        out_specs=(anywhere,) * 4,
        scratch_shapes=[dma((4,))],
    )(*made)
    return bo.reshape(inputs.shape), ig.reshape(inputs.shape), gg.reshape(width), bb


def solution(mesh):
    return jax.shard_map(
        functools.partial(per_device, dict(mesh.shape)),
        mesh=mesh,
        in_specs=(
            P("dp", None, "space", "tm"),
            P("dp", None, "space", "tm"),
            P(),
            P("tm", None),
            P(None, "tm"),
            P(None, "tm"),
            P(None, "tm"),
            P("tm", None),
        ),
        out_specs=(
            P("dp", None, "space", "tm"),
            P("dp", None, "space", "tm"),
            P("tm"),
            P("tm", None),
        ),
        check_vma=False,
    )
```

```python
import functools

import jax
import jax.numpy as jnp
from jax import lax
from jax.experimental import pallas as pl
from jax.experimental.pallas import tpu as pltpu
from jax.sharding import PartitionSpec as P

F32 = jnp.float32
BF16 = jnp.bfloat16
I32 = jnp.int32
NEG = -1e30
LANES = 128


def nn(a, b, precision=None):
    return lax.dot_general(
        a, b, (((1,), (0,)), ((), ())), precision=precision, preferred_element_type=F32
    )


def nt(a, b, precision=None):
    return lax.dot_general(
        a, b, (((1,), (1,)), ((), ())), precision=precision, preferred_element_type=F32
    )


def iota(shape, dim):
    return lax.broadcasted_iota(I32, shape, dim)


def onehot_rows(rows, cols, per):
    return (lax.div(iota((rows, cols), 0), per) == iota((rows, cols), 1)).astype(F32)


def onehot_cols(rows, cols, per):
    return (lax.div(iota((rows, cols), 1), per) == iota((rows, cols), 0)).astype(F32)


def kernel(
    cfg,
    x_hbm,
    g_hbm,
    gain_hbm,
    bias_hbm,
    wq_hbm,
    wk_hbm,
    wv_hbm,
    wo_hbm,
    bo_ref,
    ig_ref,
    gg_ref,
    bb_ref,
    x_all,
    g_all,
    w_all,
    wo,
    gain,
    bias,
    bm,
    probs,
    xg,
    qm,
    km,
    vm,
    gam,
    ks,
    vs,
    q_t,
    ga_t,
    sinv,
    att,
    gq_acc,
    gk_t,
    gv_t,
    gcat,
    gsum,
    mix_own,
    mix_opp,
    mix_dir,
    mix_part,
    mix_sum,
    mix_ropp,
    mix_rdir,
    mix_rsum,
    ig_own,
    ig_opp,
    ig_dir,
    ig_part,
    ig_sum,
    ig_ropp,
    ig_rdir,
    ig_rsum,
    slices,
    slices_recv,
    pay0,
    pay0_recv,
    pay1,
    mid_recv,
    pay2,
    far_recv,
    back,
    lsem,
    xsend,
    xrecv,
    gsend,
    grecv,
    msend,
    mrecv,
    isend,
    irecv,
    ssend,
    srecv,
    csend,
    crecv,
    nsend,
    nrecv,
    fsend,
    frecv,
):
    frames, pixels, heads, n, xs, za_lo, za_hi, zb, cores = cfg
    rows, width = x_hbm.shape
    chans = width * n
    head_dim = width // heads
    scale = head_dim ** (-0.5)
    half = rows // 2
    lo, hi = pl.ds(0, half), pl.ds(half, half)
    me = lax.axis_index("tm")
    dp = lax.axis_index("dp")
    sp = lax.axis_index("space")
    my_core = lax.rem(sp, cores)
    run = lax.rem(dp, za_lo * zb)
    my_x, my_zb = lax.div(dp, za_lo * zb), lax.rem(run, zb)
    my_za = lax.div(sp, cores) * za_lo + lax.div(run, zb)

    def device(x, a, b, core, y):
        return (
            (x * za_lo + lax.rem(a, za_lo)) * zb + b,
            lax.div(a, za_lo) * cores + core,
            y,
        )

    shard = [lax.rem(me + a, n) for a in range(n)]
    ring = [(dp, sp, shard[a]) for a in range(n)]
    slice_to = [
        (a, device(my_x, my_za, my_zb, lax.rem(my_core + c, cores), shard[a]))
        for a in (2, 1, 3)
        for c in range(cores)
    ]
    twins = [
        device(my_x, my_za, my_zb, lax.rem(my_core + c, cores), me) for c in range(1, cores)
    ]
    mid = [
        device(lax.rem(my_x + b, xs), my_za, lax.rem(my_zb + d, zb), my_core, me)
        for b in range(xs)
        for d in range(zb)
        if b or d
    ]
    far = [
        device(my_x, lax.rem(my_za + a, za_lo * za_hi), my_zb, my_core, me)
        for a in range(1, za_lo * za_hi)
    ]

    def send(src, dst, ssem, rsem, to):
        return pltpu.make_async_remote_copy(
            src_ref=src,
            dst_ref=dst,
            send_sem=ssem,
            recv_sem=rsem,
            device_id=to,
            device_id_type=pl.DeviceIdType.MESH,
        )

    def gather(src, dst, ssem, rsem):
        moves = [
            (src.at[lo], dst.at[me, lo], 1),
            (src.at[hi], dst.at[me, hi], 3),
            (src.at[hi], dst.at[me, hi], 1),
            (src.at[lo], dst.at[me, lo], 3),
            (dst.at[shard[3], lo], dst.at[shard[3], lo], 1),
            (dst.at[shard[1], hi], dst.at[shard[1], hi], 3),
        ]
        return [
            send(s, d, ssem.at[i], rsem.at[i], ring[a]) for i, (s, d, a) in enumerate(moves)
        ]

    def scatter(opp, direct, total, ropp, rdir, rsum, ssem, rsem):
        moves = [
            (opp.at[lo], ropp.at[0], 1),
            (opp.at[hi], ropp.at[1], 3),
            (direct.at[0], rdir.at[0], 3),
            (direct.at[1], rdir.at[1], 1),
            (total.at[0], rsum.at[0], 1),
            (total.at[1], rsum.at[1], 3),
        ]
        return [
            send(s, d, ssem.at[i], rsem.at[i], ring[a]) for i, (s, d, a) in enumerate(moves)
        ]

    def cols(a):
        return pl.ds(pl.multiple_of(shard[a] * width, width), width)

    loads = [
        pltpu.make_async_copy(bias_hbm, bias, lsem.at[2]),
        pltpu.make_async_copy(x_hbm, x_all.at[me], lsem.at[0]),
        pltpu.make_async_copy(gain_hbm, gain, lsem.at[1]),
        pltpu.make_async_copy(wq_hbm, w_all.at[:, pl.ds(0, width)], lsem.at[3]),
        pltpu.make_async_copy(wk_hbm, w_all.at[:, pl.ds(width, width)], lsem.at[4]),
        pltpu.make_async_copy(wv_hbm, w_all.at[:, pl.ds(2 * width, width)], lsem.at[5]),
        pltpu.make_async_copy(wo_hbm, wo, lsem.at[6]),
        pltpu.make_async_copy(g_hbm, g_all.at[me], lsem.at[7]),
    ]
    for load in loads:
        load.start()

    barrier = pltpu.get_barrier_semaphore()
    peers = [to for _, to in slice_to] + twins + mid + far
    for peer in peers:
        pl.semaphore_signal(
            barrier, inc=1, device_id=peer, device_id_type=pl.DeviceIdType.MESH
        )

    loads[0].wait()
    by_row = onehot_rows(rows, 32, pixels).astype(BF16)
    by_col = onehot_cols(LANES, rows, pixels).astype(BF16)
    by_col = jnp.concatenate([by_col, by_col], axis=0)
    same = lax.rem(iota((rows, rows), 0), pixels) == lax.rem(iota((rows, rows), 1), pixels)
    offs = 2 * frames - 1
    ahead = lax.rem(iota((offs, LANES), 1) + (frames - 1), LANES)
    spread = (iota((offs, LANES), 0) == ahead).astype(F32)
    wide = nn(bias[...], spread, lax.Precision.HIGHEST)

    def bias_table(h):
        line = jnp.broadcast_to(wide[h : h + 1, :], (32, LANES))
        table = pltpu.roll(line, 0, 1, stride=1, stride_axis=0)
        high = table.astype(BF16)
        low = (table - high.astype(F32)).astype(BF16)
        tall = nn(by_row, jnp.concatenate([high, low], axis=1)).astype(BF16)
        bm[h] = jnp.where(same, nn(tall, by_col), NEG)

    for h in range(heads // 2):
        bias_table(h)

    pl.semaphore_wait(barrier, len(peers))

    x_out = gather(x_hbm, x_all, xsend, xrecv)
    g_out = gather(g_hbm, g_all, gsend, grecv)
    for copy in x_out[:4]:
        copy.start()
    for h in range(heads // 2, heads):
        bias_table(h)
    for load in loads[1:]:
        load.wait()

    def take(a, square):
        part = x_all[shard[a]].astype(F32)
        xg[:, cols(a)] = (part * gain[:, cols(a)]).astype(BF16)
        return square + jnp.sum(part * part, axis=1, keepdims=True)

    square = take(0, jnp.zeros((rows, 1), F32))
    x_out[0].wait_recv()
    x_out[4].start()
    x_out[1].wait_recv()
    x_out[5].start()
    for copy in g_out[:4]:
        copy.start()
    x_out[2].wait_recv()
    square = take(3, square)
    x_out[3].wait_recv()
    square = take(1, square)
    x_out[4].wait_recv()
    x_out[5].wait_recv()
    square = take(2, square)
    inv = lax.rsqrt(square * (1.0 / chans) + 1e-06)
    sinv[...] = jnp.broadcast_to(inv, (rows, LANES))

    head_of = lax.div(iota((rows, width), 1), head_dim)
    eye = (iota((width, width), 0) == iota((width, width), 1)).astype(BF16)

    qkv = nn(xg[...], w_all[...]) * inv
    q = (qkv[:, :width].astype(BF16).astype(F32) * scale).astype(BF16)
    k = qkv[:, width : 2 * width].astype(BF16)
    v = qkv[:, 2 * width :].astype(BF16)
    ks[...] = k
    vs[...] = v
    q_t[...] = nt(eye, q).astype(BF16)
    for h in range(heads):
        qm[h] = jnp.where(head_of == h, q.astype(F32), 0.0).astype(BF16)
        km[h] = jnp.where(head_of == h, k.astype(F32), 0.0).astype(BF16)
        vm[h] = jnp.where(head_of == h, v.astype(F32), 0.0).astype(BF16)

    att[...] = jnp.zeros((rows, width), F32)
    for h in range(heads):
        scores = nt(qm[h], ks[...]) + bm[h]
        top = jnp.max(scores, axis=1, keepdims=True)
        e = jnp.exp(scores - top)
        total = jnp.sum(e, axis=1, keepdims=True)
        p = (e * (1.0 / total)).astype(BF16)
        probs[h] = p
        att[...] += nn(p, vm[h])
        if h == 0:
            g_out[0].wait_recv()
            g_out[4].start()
            g_out[1].wait_recv()
            g_out[5].start()

    att_b = att[...].astype(BF16)
    m_out = scatter(mix_opp, mix_dir, mix_sum, mix_ropp, mix_rdir, mix_rsum, msend, mrecv)
    mix_opp[...] = nn(att_b, wo[:, cols(2)]).astype(BF16)
    m_out[0].start()
    m_out[1].start()
    part = nn(att_b, wo[:, cols(3)])
    mix_dir[0] = part[:half].astype(BF16)
    mix_part[1] = part[half:]
    m_out[2].start()
    part = nn(att_b, wo[:, cols(1)])
    mix_part[0] = part[:half]
    mix_dir[1] = part[half:].astype(BF16)
    m_out[3].start()
    mix_own[...] = nn(att_b, wo[:, cols(0)])

    ga_f = nt(g_all[me], wo[:, cols(0)])
    g_out[2].wait_recv()
    ga_f = ga_f + nt(g_all[shard[3]], wo[:, cols(3)])
    g_out[3].wait_recv()
    ga_f = ga_f + nt(g_all[shard[1]], wo[:, cols(1)])
    g_out[4].wait_recv()
    g_out[5].wait_recv()
    ga_f = ga_f + nt(g_all[shard[2]], wo[:, cols(2)])
    ga = ga_f.astype(BF16)
    ga_t[...] = nt(eye, ga).astype(BF16)
    for h in range(heads):
        gam[h] = jnp.where(head_of == h, ga.astype(F32), 0.0).astype(BF16)

    last_first = (
        lax.div(iota((32, rows), 1), pixels) == (frames - 1) - iota((32, rows), 0)
    ).astype(BF16)
    gq_acc[...] = jnp.zeros((rows, width), F32)
    for h in range(heads):
        at = pl.ds(h * head_dim, head_dim)
        p = probs[h].astype(F32)
        grad_p = nt(gam[h], vs[...])
        dot = jnp.sum(p * grad_p, axis=1, keepdims=True)
        grad_s = (p * (grad_p - dot)).astype(BF16)
        gq_acc[...] += nn(grad_s, km[h])
        gk_t[at, :] = nn(q_t[at, :], grad_s).astype(BF16)
        gv_t[at, :] = nn(ga_t[at, :], probs[h]).astype(BF16)
        gsum[h] = nn(last_first, grad_s)

    eye_r = (iota((rows, rows), 0) == iota((rows, rows), 1)).astype(BF16)
    gq = (gq_acc[...] * scale).astype(BF16)
    gk_f = nt(eye_r, gk_t[...])
    gv_f = nt(eye_r, gv_t[...])
    gcat[:, :width] = gq
    gcat[:, width : 2 * width] = gk_f.astype(BF16)
    gcat[:, 2 * width :] = gv_f.astype(BF16)
    inv = sinv[:, :1]

    s_out = [
        send(slices.at[a - 1], slices_recv.at[j], ssend.at[j], srecv.at[j], to)
        for j, (a, to) in enumerate(slice_to)
    ]
    for a in (2, 1, 3, 0):
        back[a] = nt(gcat[...], w_all[cols(a), :])
        gain_part = jnp.sum(back[a] * (x_all[shard[a]].astype(F32) * inv), axis=0, keepdims=True)
        if a:
            slices[a - 1] = gain_part
            for j, (b, _) in enumerate(slice_to):
                if a == b:
                    s_out[j].start()
        else:
            pay0[:, :width] = gain_part
    by_key = onehot_rows(rows, LANES, pixels)
    for h in range(0, heads, 2):
        pair = jnp.zeros((1, LANES), F32)
        for side in range(2):
            pairs = nn(gsum[h + side], by_key, lax.Precision.HIGHEST)
            moved = pltpu.roll(pairs, 0, 1, stride=1, stride_axis=0)
            line = jnp.sum(moved, axis=0, keepdims=True)
            pair = pair + (pltpu.roll(line, LANES // 2, 1) if side else line)
        pay0[:, width + LANES // 2 * h : width + LANES // 2 * (h + 2)] = pair
    c_out = [
        send(pay0, pay0_recv.at[j], csend.at[j], crecv.at[j], to) for j, to in enumerate(twins)
    ]
    for copy in c_out:
        copy.start()

    def add_opposite(out, part, ropp, total):
        for side in range(2):
            out[side].wait_recv()
            total[side] = (part[side] + ropp[side].astype(F32)).astype(BF16)
            out[4 + side].start()

    add_opposite(m_out, mix_part, mix_ropp, mix_sum)

    qf = functools.reduce(jnp.add, [qm[h] for h in range(heads)])
    dots = (
        gq.astype(F32) * qf.astype(F32) * (1.0 / scale)
        + gk_f * ks[...].astype(F32)
        + gv_f * vs[...].astype(F32)
    )
    mean = jnp.sum(dots, axis=1, keepdims=True) * (inv * inv * (1.0 / chans))
    i_out = scatter(ig_opp, ig_dir, ig_sum, ig_ropp, ig_rdir, ig_rsum, isend, irecv)

    def share(a):
        part = x_all[shard[a]].astype(F32)
        return back[a] * (gain[:, cols(a)] * inv) - part * mean

    ig_opp[...] = share(2).astype(BF16)
    i_out[0].start()
    i_out[1].start()

    total = pay0[...]
    for j, copy in enumerate(c_out):
        copy.wait_recv()
        total = total + pay0_recv[j]
    pay1[...] = total
    for j, copy in enumerate(s_out):
        copy.wait_recv()
        pay1[:, :width] += slices_recv[j]
    n_out = [
        send(pay1, mid_recv.at[j], nsend.at[j], nrecv.at[j], peer) for j, peer in enumerate(mid)
    ]
    for copy in n_out:
        copy.start()

    part = share(3)
    ig_dir[0] = part[:half].astype(BF16)
    ig_part[1] = part[half:]
    i_out[2].start()
    part = share(1)
    ig_part[0] = part[:half]
    ig_dir[1] = part[half:].astype(BF16)
    i_out[3].start()
    ig_own[...] = share(0)

    def finish(first, own, out, rdir, rsum, staged):
        for copy in out[2:]:
            copy.wait_recv()
        for side in range(2):
            at = pl.ds(side * half, half)
            got = rdir[side].astype(F32) + rsum[side].astype(F32)
            staged[at, :] = (first[me, at].astype(F32) + own[at, :] + got).astype(BF16)

    add_opposite(i_out, ig_part, ig_ropp, ig_sum)
    total = pay1[...]
    for j, copy in enumerate(n_out):
        copy.wait_recv()
        total = total + mid_recv[j]
    pay2[...] = total
    f_out = [
        send(pay2, far_recv.at[j], fsend.at[j], frecv.at[j], peer) for j, peer in enumerate(far)
    ]
    for copy in f_out:
        copy.start()

    finish(x_all, mix_own, m_out, mix_rdir, mix_rsum, bo_ref)
    finish(g_all, ig_own, i_out, ig_rdir, ig_rsum, ig_ref)
    for copy in x_out + g_out + m_out + i_out + s_out + c_out + n_out:
        copy.wait_send()

    total = pay2[...]
    for j, copy in enumerate(f_out):
        copy.wait_recv()
        total = total + far_recv[j]
    gg_ref[...] = total[:, :width]
    for h in range(heads):
        first = width + LANES // 2 * h
        bb_ref[h : h + 1, :] = total[:, first : first + offs]
    for copy in f_out:
        copy.wait_send()


def hand_over(*refs):
    count = (len(refs) - 1) // 2
    copies = [
        pltpu.make_async_copy(src, dst, refs[-1].at[i])
        for i, (src, dst) in enumerate(zip(refs[:count], refs[count:-1]))
    ]
    for copy in copies:
        copy.start()
    for copy in copies:
        copy.wait()


def per_device(mesh_shape, inputs, out_grad, norm_gain, pos_bias, w_query, w_key, w_value, w_out):
    clips, frames, pixels, width = inputs.shape
    heads = pos_bias.shape[0]
    n = mesh_shape["tm"]
    chans = width * n
    rows = clips * frames * pixels
    half = rows // 2
    cores, zb = 2, 4 if mesh_shape["dp"] % 8 == 0 else 1
    za_lo = 2 if mesh_shape["dp"] % 8 == 0 else 1
    xs, za_hi = mesh_shape["dp"] // (za_lo * zb), mesh_shape["space"] // cores
    mid, far = max(1, xs * zb - 1), max(1, za_lo * za_hi - 1)
    pay = width + LANES // 2 * heads
    cfg = (frames, pixels, heads, n, xs, za_lo, za_hi, zb, cores)
    vmem, dma = pltpu.VMEM, pltpu.SemaphoreType.DMA
    anywhere = pl.BlockSpec(memory_space=pl.ANY)
    in_vmem = pl.BlockSpec(memory_space=pltpu.VMEM)
    sums = [
        vmem((rows, width), F32),
        vmem((rows, width), BF16),
        vmem((2, half, width), BF16),
        vmem((2, half, width), F32),
    ] + [vmem((2, half, width), BF16)] * 4
    results = (
        jax.ShapeDtypeStruct((rows, width), BF16),
        jax.ShapeDtypeStruct((rows, width), BF16),
        jax.ShapeDtypeStruct((1, width), F32),
        jax.ShapeDtypeStruct(pos_bias.shape, F32),
    )
    made = pl.pallas_call(
        functools.partial(kernel, cfg),
        out_shape=tuple(vmem(r.shape, r.dtype) for r in results),
        in_specs=[anywhere] * 8,
        out_specs=(in_vmem,) * 4,
        scratch_shapes=[
            vmem((n, rows, width), BF16),
            vmem((n, rows, width), BF16),
            vmem((chans, 3 * width), BF16),
            vmem((width, chans), BF16),
            vmem((1, chans), F32),
            vmem(pos_bias.shape, F32),
            vmem((heads, rows, rows), F32),
            vmem((heads, rows, rows), BF16),
            vmem((rows, chans), BF16),
            vmem((heads, rows, width), BF16),
            vmem((heads, rows, width), BF16),
            vmem((heads, rows, width), BF16),
            vmem((heads, rows, width), BF16),
            vmem((rows, width), BF16),
            vmem((rows, width), BF16),
            vmem((width, rows), BF16),
            vmem((width, rows), BF16),
            vmem((rows, LANES), F32),
            vmem((rows, width), F32),
            vmem((rows, width), F32),
            vmem((width, rows), BF16),
            vmem((width, rows), BF16),
            vmem((rows, 3 * width), BF16),
            vmem((heads, 32, rows), F32),
        ]
        + sums
        + sums
        + [
            vmem((n - 1, 1, width), F32),
            vmem(((n - 1) * cores, 1, width), F32),
            vmem((1, pay), F32),
            vmem((cores - 1, 1, pay), F32),
            vmem((1, pay), F32),
            vmem((mid, 1, pay), F32),
            vmem((1, pay), F32),
            vmem((far, 1, pay), F32),
            vmem((n, rows, width), F32),
            dma((8,)),
        ]
        + [dma((6,))] * 8
        + [dma(((n - 1) * cores,))] * 2
        + [dma((cores - 1,))] * 2
        + [dma((mid,))] * 2
        + [dma((far,))] * 2,
        compiler_params=pltpu.CompilerParams(
            collective_id=0, has_side_effects=True, vmem_limit_bytes=56 * 1024 * 1024
        ),
    )(
        inputs.reshape(rows, width),
        out_grad.reshape(rows, width),
        norm_gain.reshape(1, chans),
        pos_bias,
        w_query,
        w_key,
        w_value,
        w_out,
    )
    bo, ig, gg, bb = pl.pallas_call(
        hand_over,
        out_shape=results,
        in_specs=[in_vmem] * 4,
        out_specs=(anywhere,) * 4,
        scratch_shapes=[dma((4,))],
    )(*[pltpu.with_memory_space_constraint(m, pltpu.VMEM) for m in made])
    return bo.reshape(inputs.shape), ig.reshape(inputs.shape), gg.reshape(width), bb


def solution(mesh):
    return jax.shard_map(
        functools.partial(per_device, dict(mesh.shape)),
        mesh=mesh,
        in_specs=(
            P("dp", None, "space", "tm"),
            P("dp", None, "space", "tm"),
            P(),
            P("tm", None),
            P(None, "tm"),
            P(None, "tm"),
            P(None, "tm"),
            P("tm", None),
        ),
        out_specs=(
            P("dp", None, "space", "tm"),
            P("dp", None, "space", "tm"),
            P("tm"),
            P("tm", None),
        ),
        check_vma=False,
    )
```

```python
import functools

import jax
import jax.numpy as jnp
from jax import lax
from jax.experimental import pallas as pl
from jax.experimental.pallas import tpu as pltpu
from jax.sharding import PartitionSpec as P

F32 = jnp.float32
BF16 = jnp.bfloat16
I32 = jnp.int32
NEG = -1e30
LANES = 128


def nn(a, b, precision=None):
    return lax.dot_general(
        a, b, (((1,), (0,)), ((), ())), precision=precision, preferred_element_type=F32
    )


def nt(a, b, precision=None):
    return lax.dot_general(
        a, b, (((1,), (1,)), ((), ())), precision=precision, preferred_element_type=F32
    )


def iota(shape, dim):
    return lax.broadcasted_iota(I32, shape, dim)


def onehot_rows(rows, cols, per):
    return (lax.div(iota((rows, cols), 0), per) == iota((rows, cols), 1)).astype(F32)


def onehot_cols(rows, cols, per):
    return (lax.div(iota((rows, cols), 1), per) == iota((rows, cols), 0)).astype(F32)


def kernel(
    cfg,
    x_hbm,
    g_hbm,
    gain_hbm,
    bias_hbm,
    wq_hbm,
    wk_hbm,
    wv_hbm,
    wo_hbm,
    bo_ref,
    ig_ref,
    gg_ref,
    bb_ref,
    x_all,
    g_all,
    w_all,
    wo,
    gain,
    bias,
    bm,
    probs,
    xg,
    qm,
    km,
    vm,
    gam,
    ks,
    vs,
    q_t,
    ga_t,
    sinv,
    att,
    gq_acc,
    gk_t,
    gv_t,
    gcat,
    gsum,
    mix_own,
    mix_opp,
    mix_dir,
    mix_part,
    mix_sum,
    mix_ropp,
    mix_rdir,
    mix_rsum,
    ig_own,
    ig_opp,
    ig_dir,
    ig_part,
    ig_sum,
    ig_ropp,
    ig_rdir,
    ig_rsum,
    slices,
    slices_recv,
    pay0,
    pay0_recv,
    pay1,
    mid_recv,
    pay2,
    far_recv,
    back,
    scaled,
    lsem,
    xsend,
    xrecv,
    gsend,
    grecv,
    msend,
    mrecv,
    isend,
    irecv,
    ssend,
    srecv,
    csend,
    crecv,
    nsend,
    nrecv,
    fsend,
    frecv,
):
    frames, pixels, heads, n, xs, za_lo, za_hi, zb, cores = cfg
    rows, width = x_hbm.shape
    chans = width * n
    head_dim = width // heads
    scale = head_dim ** (-0.5)
    half = rows // 2
    lo, hi = pl.ds(0, half), pl.ds(half, half)
    me = lax.axis_index("tm")
    dp = lax.axis_index("dp")
    sp = lax.axis_index("space")
    my_core = lax.rem(sp, cores)
    run = lax.rem(dp, za_lo * zb)
    my_x, my_zb = lax.div(dp, za_lo * zb), lax.rem(run, zb)
    my_za = lax.div(sp, cores) * za_lo + lax.div(run, zb)

    def device(x, a, b, core, y):
        return (
            (x * za_lo + lax.rem(a, za_lo)) * zb + b,
            lax.div(a, za_lo) * cores + core,
            y,
        )

    shard = [lax.rem(me + a, n) for a in range(n)]
    ring = [(dp, sp, shard[a]) for a in range(n)]
    slice_to = [
        (a, device(my_x, my_za, my_zb, lax.rem(my_core + c, cores), shard[a]))
        for a in (2, 1, 3)
        for c in range(cores)
    ]
    twins = [
        device(my_x, my_za, my_zb, lax.rem(my_core + c, cores), me) for c in range(1, cores)
    ]
    mid = [
        device(lax.rem(my_x + b, xs), my_za, lax.rem(my_zb + d, zb), my_core, me)
        for b in range(xs)
        for d in range(zb)
        if b or d
    ]
    far = [
        device(my_x, lax.rem(my_za + a, za_lo * za_hi), my_zb, my_core, me)
        for a in range(1, za_lo * za_hi)
    ]

    def send(src, dst, ssem, rsem, to):
        return pltpu.make_async_remote_copy(
            src_ref=src,
            dst_ref=dst,
            send_sem=ssem,
            recv_sem=rsem,
            device_id=to,
            device_id_type=pl.DeviceIdType.MESH,
        )

    def gather(src, dst, ssem, rsem):
        piece = [pl.ds(i * (rows // 4), rows // 4) for i in range(4)]
        moves = [
            (src.at[piece[0]], dst.at[me, piece[0]], 1),
            (src.at[piece[2]], dst.at[me, piece[2]], 3),
            (src.at[piece[1]], dst.at[me, piece[1]], 1),
            (src.at[piece[3]], dst.at[me, piece[3]], 3),
            (src.at[hi], dst.at[me, hi], 1),
            (src.at[lo], dst.at[me, lo], 3),
            (dst.at[shard[3], piece[0]], dst.at[shard[3], piece[0]], 1),
            (dst.at[shard[1], piece[2]], dst.at[shard[1], piece[2]], 3),
            (dst.at[shard[3], piece[1]], dst.at[shard[3], piece[1]], 1),
            (dst.at[shard[1], piece[3]], dst.at[shard[1], piece[3]], 3),
        ]
        return [
            send(s, d, ssem.at[i], rsem.at[i], ring[a]) for i, (s, d, a) in enumerate(moves)
        ]

    def pass_on(out, which):
        for i in which:
            out[i].wait_recv()
            out[6 + i].start()

    def scatter(opp, direct, total, ropp, rdir, rsum, ssem, rsem):
        moves = [
            (opp.at[lo], ropp.at[0], 1),
            (opp.at[hi], ropp.at[1], 3),
            (direct.at[0], rdir.at[0], 3),
            (direct.at[1], rdir.at[1], 1),
            (total.at[0], rsum.at[0], 1),
            (total.at[1], rsum.at[1], 3),
        ]
        return [
            send(s, d, ssem.at[i], rsem.at[i], ring[a]) for i, (s, d, a) in enumerate(moves)
        ]

    def cols(a):
        return pl.ds(pl.multiple_of(shard[a] * width, width), width)

    barrier = pltpu.get_barrier_semaphore()
    peers = mid + [to for _, to in slice_to] + twins + far
    for peer in peers:
        pl.semaphore_signal(
            barrier, inc=1, device_id=peer, device_id_type=pl.DeviceIdType.MESH
        )

    loads = [
        pltpu.make_async_copy(bias_hbm, bias, lsem.at[2]),
        pltpu.make_async_copy(x_hbm, x_all.at[me], lsem.at[0]),
        pltpu.make_async_copy(gain_hbm, gain, lsem.at[1]),
        pltpu.make_async_copy(wq_hbm, w_all.at[0], lsem.at[3]),
        pltpu.make_async_copy(wk_hbm, w_all.at[1], lsem.at[4]),
        pltpu.make_async_copy(wv_hbm, w_all.at[2], lsem.at[5]),
        pltpu.make_async_copy(wo_hbm, wo, lsem.at[6]),
        pltpu.make_async_copy(g_hbm, g_all.at[me], lsem.at[7]),
    ]
    for load in loads:
        load.start()

    loads[0].wait()
    by_row = onehot_rows(rows, 32, pixels).astype(BF16)
    by_col = onehot_cols(LANES, rows, pixels).astype(BF16)
    by_col = jnp.concatenate([by_col, by_col], axis=0)
    same = lax.rem(iota((rows, rows), 0), pixels) == lax.rem(iota((rows, rows), 1), pixels)
    offs = 2 * frames - 1
    ahead = lax.rem(iota((offs, LANES), 1) + (frames - 1), LANES)
    spread = (iota((offs, LANES), 0) == ahead).astype(F32)
    wide = nn(bias[...], spread, lax.Precision.HIGHEST)

    def bias_table(h):
        line = jnp.broadcast_to(wide[h : h + 1, :], (32, LANES))
        table = pltpu.roll(line, 0, 1, stride=1, stride_axis=0)
        high = table.astype(BF16)
        low = (table - high.astype(F32)).astype(BF16)
        tall = nn(by_row, jnp.concatenate([high, low], axis=1)).astype(BF16)
        bm[h] = jnp.where(same, nn(tall, by_col), NEG)

    for h in range(heads // 2):
        bias_table(h)

    pl.semaphore_wait(barrier, len(peers))

    x_out = gather(x_hbm, x_all, xsend, xrecv)
    g_out = gather(g_hbm, g_all, gsend, grecv)
    for copy in x_out[:6]:
        copy.start()
    for h in range(heads // 2, heads):
        bias_table(h)
    def take(a, square):
        part = x_all[shard[a]].astype(F32)
        xg[:, cols(a)] = (part * gain[:, cols(a)]).astype(BF16)
        return square + jnp.sum(part * part, axis=1, keepdims=True)

    pass_on(x_out, range(4))
    for copy in g_out[:6]:
        copy.start()
    for load in loads[1:]:
        load.wait()
    square = take(0, jnp.zeros((rows, 1), F32))
    x_out[4].wait_recv()
    square = take(3, square)
    x_out[5].wait_recv()
    square = take(1, square)
    for copy in x_out[6:]:
        copy.wait_recv()
    square = take(2, square)
    inv = lax.rsqrt(square * (1.0 / chans) + 1e-06)
    sinv[...] = jnp.broadcast_to(inv, (rows, LANES))

    head_of = lax.div(iota((rows, LANES), 1), head_dim)
    pair = [slice(h // 2 * LANES, h // 2 * LANES + LANES) for h in range(heads)]

    def alone(a, h):
        return jnp.where(head_of == h % 2, a[:, pair[h]].astype(F32), 0.0).astype(BF16)

    eye = (iota((width, width), 0) == iota((width, width), 1)).astype(BF16)

    q = ((nn(xg[...], w_all[0]) * inv).astype(BF16).astype(F32) * scale).astype(BF16)
    k = (nn(xg[...], w_all[1]) * inv).astype(BF16)
    v = (nn(xg[...], w_all[2]) * inv).astype(BF16)
    ks[...] = k
    vs[...] = v
    q_t[...] = nt(eye, q).astype(BF16)
    for h in range(heads):
        qm[h] = alone(q, h)
        km[h] = alone(k, h)
        vm[h] = alone(v, h)

    for h in range(heads):
        scores = nt(qm[h], ks[:, pair[h]]) + bm[h]
        top = jnp.max(scores, axis=1, keepdims=True)
        e = jnp.exp(scores - top)
        total = jnp.sum(e, axis=1, keepdims=True)
        p = (e * (1.0 / total)).astype(BF16)
        probs[h] = p
        if h % 2:
            att[:, pair[h]] += nn(p, vm[h])
        else:
            att[:, pair[h]] = nn(p, vm[h])
        if h < 2:
            pass_on(g_out, (2 * h, 2 * h + 1))

    att_b = att[...].astype(BF16)
    m_out = scatter(mix_opp, mix_dir, mix_sum, mix_ropp, mix_rdir, mix_rsum, msend, mrecv)
    mix_opp[...] = nn(att_b, wo[:, cols(2)]).astype(BF16)
    m_out[0].start()
    m_out[1].start()
    part = nn(att_b, wo[:, cols(3)])
    mix_dir[0] = part[:half].astype(BF16)
    mix_part[1] = part[half:]
    m_out[2].start()
    part = nn(att_b, wo[:, cols(1)])
    mix_part[0] = part[:half]
    mix_dir[1] = part[half:].astype(BF16)
    m_out[3].start()
    mix_own[...] = nn(att_b, wo[:, cols(0)])

    inv = sinv[:, :1]
    for a in range(n):
        scaled[a] = x_all[shard[a]].astype(F32) * inv

    ga_f = nt(g_all[me], wo[:, cols(0)])
    g_out[4].wait_recv()
    ga_f = ga_f + nt(g_all[shard[3]], wo[:, cols(3)])
    g_out[5].wait_recv()
    ga_f = ga_f + nt(g_all[shard[1]], wo[:, cols(1)])
    for copy in g_out[6:]:
        copy.wait_recv()
    ga_f = ga_f + nt(g_all[shard[2]], wo[:, cols(2)])
    ga = ga_f.astype(BF16)
    ga_t[...] = nt(eye, ga).astype(BF16)
    for h in range(heads):
        gam[h] = alone(ga, h)

    last_first = (
        lax.div(iota((32, rows), 1), pixels) == (frames - 1) - iota((32, rows), 0)
    ).astype(BF16)
    for h in range(heads):
        at = pl.ds(h * head_dim, head_dim)
        p = probs[h].astype(F32)
        grad_p = nt(gam[h], vs[:, pair[h]])
        dot = jnp.sum(gam[h].astype(F32) * att[:, pair[h]], axis=1, keepdims=True)
        grad_s = (p * (grad_p - dot)).astype(BF16)
        if h % 2:
            gq_acc[:, pair[h]] += nn(grad_s, km[h])
        else:
            gq_acc[:, pair[h]] = nn(grad_s, km[h])
        gk_t[at, :] = nn(q_t[at, :], grad_s).astype(BF16)
        gv_t[at, :] = nn(ga_t[at, :], probs[h]).astype(BF16)
        gsum[h] = nn(last_first, grad_s)

    eye_r = (iota((rows, rows), 0) == iota((rows, rows), 1)).astype(BF16)
    gq = (gq_acc[...] * scale).astype(BF16)
    gk_f = nt(eye_r, gk_t[...])
    gv_f = nt(eye_r, gv_t[...])
    gcat[:, :width] = gq
    gcat[:, width : 2 * width] = gk_f.astype(BF16)
    gcat[:, 2 * width :] = gv_f.astype(BF16)
    s_out = [
        send(slices.at[a - 1], slices_recv.at[j], ssend.at[j], srecv.at[j], to)
        for j, (a, to) in enumerate(slice_to)
    ]
    for a in (2, 1, 3, 0):
        back[a] = (
            nt(gcat[:, :width], w_all[0, cols(a), :])
            + nt(gcat[:, width : 2 * width], w_all[1, cols(a), :])
            + nt(gcat[:, 2 * width :], w_all[2, cols(a), :])
        )
        gain_part = jnp.sum(back[a] * scaled[a], axis=0, keepdims=True)
        if a:
            slices[a - 1] = gain_part
            for j, (b, _) in enumerate(slice_to):
                if a == b:
                    s_out[j].start()
        else:
            pay0[:, :width] = gain_part
    by_key = onehot_rows(rows, LANES, pixels)
    for h in range(0, heads, 2):
        both = jnp.zeros((1, LANES), F32)
        for side in range(2):
            pairs = nn(gsum[h + side], by_key, lax.Precision.HIGHEST)
            moved = pltpu.roll(pairs, 0, 1, stride=1, stride_axis=0)
            line = jnp.sum(moved, axis=0, keepdims=True)
            both = both + (pltpu.roll(line, LANES // 2, 1) if side else line)
        pay0[:, width + LANES // 2 * h : width + LANES // 2 * (h + 2)] = both
    c_out = [
        send(pay0, pay0_recv.at[j], csend.at[j], crecv.at[j], to) for j, to in enumerate(twins)
    ]
    for copy in c_out:
        copy.start()

    def add_opposite(out, part, ropp, total):
        for side in range(2):
            out[side].wait_recv()
            total[side] = (part[side] + ropp[side].astype(F32)).astype(BF16)
            out[4 + side].start()

    add_opposite(m_out, mix_part, mix_ropp, mix_sum)

    qf = jnp.concatenate([qm[h] + qm[h + 1] for h in range(0, heads, 2)], axis=1)
    dots = (
        gq.astype(F32) * qf.astype(F32) * (1.0 / scale)
        + gk_f * ks[...].astype(F32)
        + gv_f * vs[...].astype(F32)
    )
    mean = jnp.sum(dots, axis=1, keepdims=True) * (inv * inv * (1.0 / chans))
    i_out = scatter(ig_opp, ig_dir, ig_sum, ig_ropp, ig_rdir, ig_rsum, isend, irecv)

    def share(a):
        part = x_all[shard[a]].astype(F32)
        return back[a] * (gain[:, cols(a)] * inv) - part * mean

    ig_opp[...] = share(2).astype(BF16)
    i_out[0].start()
    i_out[1].start()

    total = pay0[...]
    for j, copy in enumerate(c_out):
        copy.wait_recv()
        total = total + pay0_recv[j]
    pay1[...] = total
    for j, copy in enumerate(s_out):
        copy.wait_recv()
        pay1[:, :width] += slices_recv[j]
    n_out = [
        send(pay1, mid_recv.at[j], nsend.at[j], nrecv.at[j], peer) for j, peer in enumerate(mid)
    ]
    for copy in n_out:
        copy.start()

    part = share(3)
    ig_dir[0] = part[:half].astype(BF16)
    ig_part[1] = part[half:]
    i_out[2].start()
    part = share(1)
    ig_part[0] = part[:half]
    ig_dir[1] = part[half:].astype(BF16)
    i_out[3].start()
    ig_own[...] = share(0)

    def finish(first, own, out, rdir, rsum, staged):
        for copy in out[2:]:
            copy.wait_recv()
        for side in range(2):
            at = pl.ds(side * half, half)
            got = rdir[side].astype(F32) + rsum[side].astype(F32)
            staged[at, :] = (first[me, at].astype(F32) + own[at, :] + got).astype(BF16)

    total = pay1[...]
    for j, copy in enumerate(n_out):
        copy.wait_recv()
        total = total + mid_recv[j]
    pay2[...] = total
    f_out = [
        send(pay2, far_recv.at[j], fsend.at[j], frecv.at[j], peer) for j, peer in enumerate(far)
    ]
    for copy in f_out:
        copy.start()

    add_opposite(i_out, ig_part, ig_ropp, ig_sum)
    finish(x_all, mix_own, m_out, mix_rdir, mix_rsum, bo_ref)
    finish(g_all, ig_own, i_out, ig_rdir, ig_rsum, ig_ref)
    for copy in x_out + g_out + m_out + i_out + s_out + c_out + n_out:
        copy.wait_send()

    total = pay2[...]
    for j, copy in enumerate(f_out):
        copy.wait_recv()
        total = total + far_recv[j]
    gg_ref[...] = total[:, :width]
    for h in range(heads):
        first = width + LANES // 2 * h
        bb_ref[h : h + 1, :] = total[:, first : first + offs]
    for copy in f_out:
        copy.wait_send()


def hand_over(*refs):
    count = (len(refs) - 1) // 2
    copies = [
        pltpu.make_async_copy(src, dst, refs[-1].at[i])
        for i, (src, dst) in enumerate(zip(refs[:count], refs[count:-1]))
    ]
    for copy in copies:
        copy.start()
    for copy in copies:
        copy.wait()


def per_device(mesh_shape, inputs, out_grad, norm_gain, pos_bias, w_query, w_key, w_value, w_out):
    clips, frames, pixels, width = inputs.shape
    heads = pos_bias.shape[0]
    n = mesh_shape["tm"]
    chans = width * n
    rows = clips * frames * pixels
    half = rows // 2
    cores, zb = 2, 4 if mesh_shape["dp"] % 8 == 0 else 1
    za_lo = 2 if mesh_shape["dp"] % 8 == 0 else 1
    xs, za_hi = mesh_shape["dp"] // (za_lo * zb), mesh_shape["space"] // cores
    mid, far = max(1, xs * zb - 1), max(1, za_lo * za_hi - 1)
    pay = width + LANES // 2 * heads
    cfg = (frames, pixels, heads, n, xs, za_lo, za_hi, zb, cores)
    vmem, dma = pltpu.VMEM, pltpu.SemaphoreType.DMA
    anywhere = pl.BlockSpec(memory_space=pl.ANY)
    in_vmem = pl.BlockSpec(memory_space=pltpu.VMEM)
    sums = [
        vmem((rows, width), F32),
        vmem((rows, width), BF16),
        vmem((2, half, width), BF16),
        vmem((2, half, width), F32),
    ] + [vmem((2, half, width), BF16)] * 4
    results = (
        jax.ShapeDtypeStruct((rows, width), BF16),
        jax.ShapeDtypeStruct((rows, width), BF16),
        jax.ShapeDtypeStruct((1, width), F32),
        jax.ShapeDtypeStruct(pos_bias.shape, F32),
    )
    made = pl.pallas_call(
        functools.partial(kernel, cfg),
        out_shape=tuple(vmem(r.shape, r.dtype) for r in results),
        in_specs=[anywhere] * 8,
        out_specs=(in_vmem,) * 4,
        scratch_shapes=[
            vmem((n, rows, width), BF16),
            vmem((n, rows, width), BF16),
            vmem((3, chans, width), BF16),
            vmem((width, chans), BF16),
            vmem((1, chans), F32),
            vmem(pos_bias.shape, F32),
            vmem((heads, rows, rows), F32),
            vmem((heads, rows, rows), BF16),
            vmem((rows, chans), BF16),
            vmem((heads, rows, LANES), BF16),
            vmem((heads, rows, LANES), BF16),
            vmem((heads, rows, LANES), BF16),
            vmem((heads, rows, LANES), BF16),
            vmem((rows, width), BF16),
            vmem((rows, width), BF16),
            vmem((width, rows), BF16),
            vmem((width, rows), BF16),
            vmem((rows, LANES), F32),
            vmem((rows, width), F32),
            vmem((rows, width), F32),
            vmem((width, rows), BF16),
            vmem((width, rows), BF16),
            vmem((rows, 3 * width), BF16),
            vmem((heads, 32, rows), F32),
        ]
        + sums
        + sums
        + [
            vmem((n - 1, 1, width), F32),
            vmem(((n - 1) * cores, 1, width), F32),
            vmem((1, pay), F32),
            vmem((cores - 1, 1, pay), F32),
            vmem((1, pay), F32),
            vmem((mid, 1, pay), F32),
            vmem((1, pay), F32),
            vmem((far, 1, pay), F32),
            vmem((n, rows, width), F32),
            vmem((n, rows, width), F32),
            dma((8,)),
        ]
        + [dma((10,))] * 4
        + [dma((6,))] * 4
        + [dma(((n - 1) * cores,))] * 2
        + [dma((cores - 1,))] * 2
        + [dma((mid,))] * 2
        + [dma((far,))] * 2,
        compiler_params=pltpu.CompilerParams(
            collective_id=0, has_side_effects=True, vmem_limit_bytes=56 * 1024 * 1024
        ),
    )(
        inputs.reshape(rows, width),
        out_grad.reshape(rows, width),
        norm_gain.reshape(1, chans),
        pos_bias,
        w_query,
        w_key,
        w_value,
        w_out,
    )
    bo, ig, gg, bb = pl.pallas_call(
        hand_over,
        out_shape=results,
        in_specs=[in_vmem] * 4,
        out_specs=(anywhere,) * 4,
        scratch_shapes=[dma((4,))],
    )(*[pltpu.with_memory_space_constraint(m, pltpu.VMEM) for m in made])
    return bo.reshape(inputs.shape), ig.reshape(inputs.shape), gg.reshape(width), bb


def solution(mesh):
    return jax.shard_map(
        functools.partial(per_device, dict(mesh.shape)),
        mesh=mesh,
        in_specs=(
            P("dp", None, "space", "tm"),
            P("dp", None, "space", "tm"),
            P(),
            P("tm", None),
            P(None, "tm"),
            P(None, "tm"),
            P(None, "tm"),
            P("tm", None),
        ),
        out_specs=(
            P("dp", None, "space", "tm"),
            P("dp", None, "space", "tm"),
            P("tm"),
            P("tm", None),
        ),
        check_vma=False,
    )
```

```python
import functools

import jax
import jax.numpy as jnp
from jax import lax
from jax.experimental import pallas as pl
from jax.experimental.pallas import tpu as pltpu
from jax.sharding import PartitionSpec as P

F32 = jnp.float32
BF16 = jnp.bfloat16
I32 = jnp.int32
NEG = -1e30
LANES = 128


def nn(a, b, precision=None):
    return lax.dot_general(
        a, b, (((1,), (0,)), ((), ())), precision=precision, preferred_element_type=F32
    )


def nt(a, b, precision=None):
    return lax.dot_general(
        a, b, (((1,), (1,)), ((), ())), precision=precision, preferred_element_type=F32
    )


def iota(shape, dim):
    return lax.broadcasted_iota(I32, shape, dim)


def onehot_rows(rows, cols, per):
    return (lax.div(iota((rows, cols), 0), per) == iota((rows, cols), 1)).astype(F32)


def onehot_cols(rows, cols, per):
    return (lax.div(iota((rows, cols), 1), per) == iota((rows, cols), 0)).astype(F32)


def kernel(
    cfg,
    x_hbm,
    g_hbm,
    gain_hbm,
    bias_hbm,
    wq_hbm,
    wk_hbm,
    wv_hbm,
    wo_hbm,
    bo_ref,
    ig_ref,
    gg_ref,
    bb_ref,
    x_all,
    g_all,
    w_all,
    wo,
    gain,
    bias,
    bm,
    probs,
    xg,
    qm,
    km,
    vm,
    gam,
    ks,
    vs,
    q_t,
    ga_t,
    sinv,
    att,
    gq_acc,
    gk_t,
    gv_t,
    gcat,
    gsum,
    mix_own,
    mix_opp,
    mix_dir,
    mix_part,
    mix_sum,
    mix_ropp,
    mix_rdir,
    mix_rsum,
    ig_own,
    ig_opp,
    ig_dir,
    ig_part,
    ig_sum,
    ig_ropp,
    ig_rdir,
    ig_rsum,
    slices,
    slices_recv,
    pay0,
    pay0_recv,
    pay1,
    mid_recv,
    pay2,
    far_recv,
    back,
    scaled,
    lsem,
    xsend,
    xrecv,
    gsend,
    grecv,
    msend,
    mrecv,
    isend,
    irecv,
    ssend,
    srecv,
    csend,
    crecv,
    nsend,
    nrecv,
    fsend,
    frecv,
):
    frames, pixels, heads, n, xs, za_lo, za_hi, zb, cores = cfg
    rows, width = x_hbm.shape
    chans = width * n
    head_dim = width // heads
    scale = head_dim ** (-0.5)
    half = rows // 2
    lo, hi = pl.ds(0, half), pl.ds(half, half)
    me = lax.axis_index("tm")
    dp = lax.axis_index("dp")
    sp = lax.axis_index("space")
    my_core = lax.rem(sp, cores)
    run = lax.rem(dp, za_lo * zb)
    my_x, my_zb = lax.div(dp, za_lo * zb), lax.rem(run, zb)
    my_za = lax.div(sp, cores) * za_lo + lax.div(run, zb)

    def device(x, a, b, core, y):
        return (
            (x * za_lo + lax.rem(a, za_lo)) * zb + b,
            lax.div(a, za_lo) * cores + core,
            y,
        )

    shard = [lax.rem(me + a, n) for a in range(n)]
    ring = [(dp, sp, shard[a]) for a in range(n)]
    slice_to = [
        (a, device(my_x, my_za, my_zb, lax.rem(my_core + c, cores), shard[a]))
        for a in (2, 1, 3)
        for c in range(cores)
    ]
    twins = [
        device(my_x, my_za, my_zb, lax.rem(my_core + c, cores), me) for c in range(1, cores)
    ]
    mid = [
        device(lax.rem(my_x + b, xs), my_za, lax.rem(my_zb + d, zb), my_core, me)
        for b in range(xs)
        for d in range(zb)
        if b or d
    ]
    far = [
        device(my_x, lax.rem(my_za + a, za_lo * za_hi), my_zb, my_core, me)
        for a in range(1, za_lo * za_hi)
    ]

    def send(src, dst, ssem, rsem, to):
        return pltpu.make_async_remote_copy(
            src_ref=src,
            dst_ref=dst,
            send_sem=ssem,
            recv_sem=rsem,
            device_id=to,
            device_id_type=pl.DeviceIdType.MESH,
        )

    def gather(src, dst, ssem, rsem):
        piece = [pl.ds(i * (rows // 4), rows // 4) for i in range(4)]
        moves = [
            (src.at[piece[0]], dst.at[me, piece[0]], 1),
            (src.at[piece[2]], dst.at[me, piece[2]], 3),
            (src.at[piece[1]], dst.at[me, piece[1]], 1),
            (src.at[piece[3]], dst.at[me, piece[3]], 3),
            (src.at[hi], dst.at[me, hi], 1),
            (src.at[lo], dst.at[me, lo], 3),
            (dst.at[shard[3], piece[0]], dst.at[shard[3], piece[0]], 1),
            (dst.at[shard[1], piece[2]], dst.at[shard[1], piece[2]], 3),
            (dst.at[shard[3], piece[1]], dst.at[shard[3], piece[1]], 1),
            (dst.at[shard[1], piece[3]], dst.at[shard[1], piece[3]], 3),
        ]
        return [
            send(s, d, ssem.at[i], rsem.at[i], ring[a]) for i, (s, d, a) in enumerate(moves)
        ]

    def pass_on(out, which):
        for i in which:
            out[i].wait_recv()
            out[6 + i].start()

    def scatter(opp, direct, total, ropp, rdir, rsum, ssem, rsem):
        moves = [
            (opp.at[lo], ropp.at[0], 1),
            (opp.at[hi], ropp.at[1], 3),
            (direct.at[0], rdir.at[0], 3),
            (direct.at[1], rdir.at[1], 1),
            (total.at[0], rsum.at[0], 1),
            (total.at[1], rsum.at[1], 3),
        ]
        return [
            send(s, d, ssem.at[i], rsem.at[i], ring[a]) for i, (s, d, a) in enumerate(moves)
        ]

    def cols(a):
        return pl.ds(pl.multiple_of(shard[a] * width, width), width)

    barrier = pltpu.get_barrier_semaphore()
    peers = far + mid + [to for _, to in slice_to] + twins
    for peer in peers:
        pl.semaphore_signal(
            barrier, inc=1, device_id=peer, device_id_type=pl.DeviceIdType.MESH
        )

    loads = [
        pltpu.make_async_copy(bias_hbm, bias, lsem.at[2]),
        pltpu.make_async_copy(x_hbm, x_all.at[me], lsem.at[0]),
        pltpu.make_async_copy(gain_hbm, gain, lsem.at[1]),
        pltpu.make_async_copy(wq_hbm, w_all.at[0], lsem.at[3]),
        pltpu.make_async_copy(wk_hbm, w_all.at[1], lsem.at[4]),
        pltpu.make_async_copy(wv_hbm, w_all.at[2], lsem.at[5]),
        pltpu.make_async_copy(wo_hbm, wo, lsem.at[6]),
        pltpu.make_async_copy(g_hbm, g_all.at[me], lsem.at[7]),
    ]
    for load in loads:
        load.start()

    loads[0].wait()
    by_row = onehot_rows(rows, 32, pixels).astype(BF16)
    by_col = onehot_cols(LANES, rows, pixels).astype(BF16)
    by_col = jnp.concatenate([by_col, by_col], axis=0)
    same = lax.rem(iota((rows, rows), 0), pixels) == lax.rem(iota((rows, rows), 1), pixels)
    offs = 2 * frames - 1
    ahead = lax.rem(iota((offs, LANES), 1) + (frames - 1), LANES)
    spread = (iota((offs, LANES), 0) == ahead).astype(F32)
    wide = nn(bias[...], spread, lax.Precision.HIGHEST)

    def bias_table(h):
        line = jnp.broadcast_to(wide[h : h + 1, :], (32, LANES))
        table = pltpu.roll(line, 0, 1, stride=1, stride_axis=0)
        high = table.astype(BF16)
        low = (table - high.astype(F32)).astype(BF16)
        tall = nn(by_row, jnp.concatenate([high, low], axis=1)).astype(BF16)
        bm[h] = jnp.where(same, nn(tall, by_col), NEG)

    for h in range(heads // 2):
        bias_table(h)

    pl.semaphore_wait(barrier, len(peers))

    x_out = gather(x_hbm, x_all, xsend, xrecv)
    g_out = gather(g_hbm, g_all, gsend, grecv)
    for copy in x_out[:6]:
        copy.start()
    for h in range(heads // 2, heads):
        bias_table(h)
    def take(a, square):
        part = x_all[shard[a]].astype(F32)
        xg[:, cols(a)] = (part * gain[:, cols(a)]).astype(BF16)
        return square + jnp.sum(part * part, axis=1, keepdims=True)

    pass_on(x_out, range(4))
    for copy in g_out[:6]:
        copy.start()
    for load in loads[1:]:
        load.wait()
    square = take(0, jnp.zeros((rows, 1), F32))
    x_out[4].wait_recv()
    square = take(3, square)
    x_out[5].wait_recv()
    square = take(1, square)
    for copy in x_out[6:]:
        copy.wait_recv()
    square = take(2, square)
    inv = lax.rsqrt(square * (1.0 / chans) + 1e-06)
    sinv[...] = jnp.broadcast_to(inv, (rows, LANES))

    head_of = lax.div(iota((rows, LANES), 1), head_dim)
    pair = [slice(h // 2 * LANES, h // 2 * LANES + LANES) for h in range(heads)]

    def alone(a, h):
        return jnp.where(head_of == h % 2, a[:, pair[h]].astype(F32), 0.0).astype(BF16)

    eye = (iota((width, width), 0) == iota((width, width), 1)).astype(BF16)

    q = ((nn(xg[...], w_all[0]) * inv).astype(BF16).astype(F32) * scale).astype(BF16)
    k = (nn(xg[...], w_all[1]) * inv).astype(BF16)
    v = (nn(xg[...], w_all[2]) * inv).astype(BF16)
    ks[...] = k
    vs[...] = v
    q_t[...] = nt(eye, q).astype(BF16)
    for h in range(heads):
        qm[h] = alone(q, h)
        km[h] = alone(k, h)
        vm[h] = alone(v, h)

    for h in range(heads):
        scores = nt(qm[h], ks[:, pair[h]]) + bm[h]
        top = jnp.max(scores, axis=1, keepdims=True)
        e = jnp.exp(scores - top)
        total = jnp.sum(e, axis=1, keepdims=True)
        p = (e * (1.0 / total)).astype(BF16)
        probs[h] = p
        if h % 2:
            att[:, pair[h]] += nn(p, vm[h])
        else:
            att[:, pair[h]] = nn(p, vm[h])
        if h < 2:
            pass_on(g_out, (2 * h, 2 * h + 1))

    att_b = att[...].astype(BF16)
    m_out = scatter(mix_opp, mix_dir, mix_sum, mix_ropp, mix_rdir, mix_rsum, msend, mrecv)
    mix_opp[...] = nn(att_b, wo[:, cols(2)]).astype(BF16)
    m_out[0].start()
    m_out[1].start()
    part = nn(att_b, wo[:, cols(3)])
    mix_dir[0] = part[:half].astype(BF16)
    mix_part[1] = part[half:]
    m_out[2].start()
    part = nn(att_b, wo[:, cols(1)])
    mix_part[0] = part[:half]
    mix_dir[1] = part[half:].astype(BF16)
    m_out[3].start()

    inv = sinv[:, :1]
    for a in range(n):
        scaled[a] = x_all[shard[a]].astype(F32) * inv

    ga_f = nt(g_all[me], wo[:, cols(0)])
    g_out[4].wait_recv()
    ga_f = ga_f + nt(g_all[shard[3]], wo[:, cols(3)])
    g_out[5].wait_recv()
    ga_f = ga_f + nt(g_all[shard[1]], wo[:, cols(1)])
    for copy in g_out[6:]:
        copy.wait_recv()
    ga_f = ga_f + nt(g_all[shard[2]], wo[:, cols(2)])
    ga = ga_f.astype(BF16)
    ga_t[...] = nt(eye, ga).astype(BF16)
    for h in range(heads):
        gam[h] = alone(ga, h)

    last_first = (
        lax.div(iota((32, rows), 1), pixels) == (frames - 1) - iota((32, rows), 0)
    ).astype(BF16)
    for h in range(heads):
        at = pl.ds(h * head_dim, head_dim)
        p = probs[h].astype(F32)
        grad_p = nt(gam[h], vs[:, pair[h]])
        dot = jnp.sum(gam[h].astype(F32) * att[:, pair[h]], axis=1, keepdims=True)
        grad_s = (p * (grad_p - dot)).astype(BF16)
        if h % 2:
            gq_acc[:, pair[h]] += nn(grad_s, km[h])
        else:
            gq_acc[:, pair[h]] = nn(grad_s, km[h])
        gk_t[at, :] = nn(q_t[at, :], grad_s).astype(BF16)
        gv_t[at, :] = nn(ga_t[at, :], probs[h]).astype(BF16)
        gsum[h] = nn(last_first, grad_s)

    eye_r = (iota((rows, rows), 0) == iota((rows, rows), 1)).astype(BF16)
    gq = (gq_acc[...] * scale).astype(BF16)
    gk_f = nt(eye_r, gk_t[...])
    gv_f = nt(eye_r, gv_t[...])
    gcat[:, :width] = gq
    gcat[:, width : 2 * width] = gk_f.astype(BF16)
    gcat[:, 2 * width :] = gv_f.astype(BF16)
    s_out = [
        send(slices.at[a - 1], slices_recv.at[j], ssend.at[j], srecv.at[j], to)
        for j, (a, to) in enumerate(slice_to)
    ]
    for a in (2, 1, 3, 0):
        back[a] = (
            nt(gcat[:, :width], w_all[0, cols(a), :])
            + nt(gcat[:, width : 2 * width], w_all[1, cols(a), :])
            + nt(gcat[:, 2 * width :], w_all[2, cols(a), :])
        )
        gain_part = jnp.sum(back[a] * scaled[a], axis=0, keepdims=True)
        if a:
            slices[a - 1] = gain_part
            for j, (b, _) in enumerate(slice_to):
                if a == b:
                    s_out[j].start()
        else:
            pay0[:, :width] = gain_part
    by_key = onehot_rows(rows, LANES, pixels)
    for h in range(0, heads, 2):
        both = jnp.zeros((1, LANES), F32)
        for side in range(2):
            pairs = nn(gsum[h + side], by_key, lax.Precision.HIGHEST)
            moved = pltpu.roll(pairs, 0, 1, stride=1, stride_axis=0)
            line = jnp.sum(moved, axis=0, keepdims=True)
            both = both + (pltpu.roll(line, LANES // 2, 1) if side else line)
        pay0[:, width + LANES // 2 * h : width + LANES // 2 * (h + 2)] = both
    c_out = [
        send(pay0, pay0_recv.at[j], csend.at[j], crecv.at[j], to) for j, to in enumerate(twins)
    ]
    for copy in c_out:
        copy.start()

    def add_opposite(out, part, ropp, total):
        for side in range(2):
            out[side].wait_recv()
            total[side] = (part[side] + ropp[side].astype(F32)).astype(BF16)
            out[4 + side].start()

    mix_own[...] = nn(att[...].astype(BF16), wo[:, cols(0)])
    add_opposite(m_out, mix_part, mix_ropp, mix_sum)

    qf = jnp.concatenate([qm[h] + qm[h + 1] for h in range(0, heads, 2)], axis=1)
    dots = (
        gq.astype(F32) * qf.astype(F32) * (1.0 / scale)
        + gk_f * ks[...].astype(F32)
        + gv_f * vs[...].astype(F32)
    )
    mean = jnp.sum(dots, axis=1, keepdims=True) * (inv * inv * (1.0 / chans))
    i_out = scatter(ig_opp, ig_dir, ig_sum, ig_ropp, ig_rdir, ig_rsum, isend, irecv)

    def share(a):
        part = x_all[shard[a]].astype(F32)
        return back[a] * (gain[:, cols(a)] * inv) - part * mean

    ig_opp[...] = share(2).astype(BF16)
    i_out[0].start()
    i_out[1].start()

    total = pay0[...]
    for j, copy in enumerate(c_out):
        copy.wait_recv()
        total = total + pay0_recv[j]
    pay1[...] = total
    for j, copy in enumerate(s_out):
        copy.wait_recv()
        pay1[:, :width] += slices_recv[j]
    n_out = [
        send(pay1, mid_recv.at[j], nsend.at[j], nrecv.at[j], peer) for j, peer in enumerate(mid)
    ]
    for copy in n_out:
        copy.start()

    part = share(3)
    ig_dir[0] = part[:half].astype(BF16)
    ig_part[1] = part[half:]
    i_out[2].start()
    part = share(1)
    ig_part[0] = part[:half]
    ig_dir[1] = part[half:].astype(BF16)
    i_out[3].start()
    ig_own[...] = share(0)

    def finish(first, own, out, rdir, rsum, staged):
        for copy in out[2:]:
            copy.wait_recv()
        for side in range(2):
            at = pl.ds(side * half, half)
            got = rdir[side].astype(F32) + rsum[side].astype(F32)
            staged[at, :] = (first[me, at].astype(F32) + own[at, :] + got).astype(BF16)

    total = pay1[...]
    for j, copy in enumerate(n_out):
        copy.wait_recv()
        total = total + mid_recv[j]
    pay2[...] = total
    f_out = [
        send(pay2, far_recv.at[j], fsend.at[j], frecv.at[j], peer) for j, peer in enumerate(far)
    ]
    for copy in f_out:
        copy.start()

    add_opposite(i_out, ig_part, ig_ropp, ig_sum)
    finish(x_all, mix_own, m_out, mix_rdir, mix_rsum, bo_ref)
    finish(g_all, ig_own, i_out, ig_rdir, ig_rsum, ig_ref)
    for copy in x_out + g_out + m_out + i_out + s_out + c_out + n_out:
        copy.wait_send()

    total = pay2[...]
    for j, copy in enumerate(f_out):
        copy.wait_recv()
        total = total + far_recv[j]
    gg_ref[...] = total[:, :width]
    for h in range(heads):
        first = width + LANES // 2 * h
        bb_ref[h : h + 1, :] = total[:, first : first + offs]
    for copy in f_out:
        copy.wait_send()


def hand_over(*refs):
    count = (len(refs) - 1) // 2
    copies = [
        pltpu.make_async_copy(src, dst, refs[-1].at[i])
        for i, (src, dst) in enumerate(zip(refs[:count], refs[count:-1]))
    ]
    for copy in copies:
        copy.start()
    for copy in copies:
        copy.wait()


def per_device(mesh_shape, inputs, out_grad, norm_gain, pos_bias, w_query, w_key, w_value, w_out):
    clips, frames, pixels, width = inputs.shape
    heads = pos_bias.shape[0]
    n = mesh_shape["tm"]
    chans = width * n
    rows = clips * frames * pixels
    half = rows // 2
    cores, zb = 2, 4 if mesh_shape["dp"] % 8 == 0 else 1
    za_lo = 2 if mesh_shape["dp"] % 8 == 0 else 1
    xs, za_hi = mesh_shape["dp"] // (za_lo * zb), mesh_shape["space"] // cores
    mid, far = max(1, xs * zb - 1), max(1, za_lo * za_hi - 1)
    pay = width + LANES // 2 * heads
    cfg = (frames, pixels, heads, n, xs, za_lo, za_hi, zb, cores)
    vmem, dma = pltpu.VMEM, pltpu.SemaphoreType.DMA
    anywhere = pl.BlockSpec(memory_space=pl.ANY)
    in_vmem = pl.BlockSpec(memory_space=pltpu.VMEM)
    sums = [
        vmem((rows, width), F32),
        vmem((rows, width), BF16),
        vmem((2, half, width), BF16),
        vmem((2, half, width), F32),
    ] + [vmem((2, half, width), BF16)] * 4
    results = (
        jax.ShapeDtypeStruct((rows, width), BF16),
        jax.ShapeDtypeStruct((rows, width), BF16),
        jax.ShapeDtypeStruct((1, width), F32),
        jax.ShapeDtypeStruct(pos_bias.shape, F32),
    )
    made = pl.pallas_call(
        functools.partial(kernel, cfg),
        out_shape=tuple(vmem(r.shape, r.dtype) for r in results),
        in_specs=[anywhere] * 8,
        out_specs=(in_vmem,) * 4,
        scratch_shapes=[
            vmem((n, rows, width), BF16),
            vmem((n, rows, width), BF16),
            vmem((3, chans, width), BF16),
            vmem((width, chans), BF16),
            vmem((1, chans), F32),
            vmem(pos_bias.shape, F32),
            vmem((heads, rows, rows), F32),
            vmem((heads, rows, rows), BF16),
            vmem((rows, chans), BF16),
            vmem((heads, rows, LANES), BF16),
            vmem((heads, rows, LANES), BF16),
            vmem((heads, rows, LANES), BF16),
            vmem((heads, rows, LANES), BF16),
            vmem((rows, width), BF16),
            vmem((rows, width), BF16),
            vmem((width, rows), BF16),
            vmem((width, rows), BF16),
            vmem((rows, LANES), F32),
            vmem((rows, width), F32),
            vmem((rows, width), F32),
            vmem((width, rows), BF16),
            vmem((width, rows), BF16),
            vmem((rows, 3 * width), BF16),
            vmem((heads, 32, rows), F32),
        ]
        + sums
        + sums
        + [
            vmem((n - 1, 1, width), F32),
            vmem(((n - 1) * cores, 1, width), F32),
            vmem((1, pay), F32),
            vmem((cores - 1, 1, pay), F32),
            vmem((1, pay), F32),
            vmem((mid, 1, pay), F32),
            vmem((1, pay), F32),
            vmem((far, 1, pay), F32),
            vmem((n, rows, width), F32),
            vmem((n, rows, width), F32),
            dma((8,)),
        ]
        + [dma((10,))] * 4
        + [dma((6,))] * 4
        + [dma(((n - 1) * cores,))] * 2
        + [dma((cores - 1,))] * 2
        + [dma((mid,))] * 2
        + [dma((far,))] * 2,
        compiler_params=pltpu.CompilerParams(
            collective_id=0, has_side_effects=True, vmem_limit_bytes=56 * 1024 * 1024
        ),
    )(
        inputs.reshape(rows, width),
        out_grad.reshape(rows, width),
        norm_gain.reshape(1, chans),
        pos_bias,
        w_query,
        w_key,
        w_value,
        w_out,
    )
    bo, ig, gg, bb = pl.pallas_call(
        hand_over,
        out_shape=results,
        in_specs=[in_vmem] * 4,
        out_specs=(anywhere,) * 4,
        scratch_shapes=[dma((4,))],
    )(*[pltpu.with_memory_space_constraint(m, pltpu.VMEM) for m in made])
    return bo.reshape(inputs.shape), ig.reshape(inputs.shape), gg.reshape(width), bb


def solution(mesh):
    return jax.shard_map(
        functools.partial(per_device, dict(mesh.shape)),
        mesh=mesh,
        in_specs=(
            P("dp", None, "space", "tm"),
            P("dp", None, "space", "tm"),
            P(),
            P("tm", None),
            P(None, "tm"),
            P(None, "tm"),
            P(None, "tm"),
            P("tm", None),
        ),
        out_specs=(
            P("dp", None, "space", "tm"),
            P("dp", None, "space", "tm"),
            P("tm"),
            P("tm", None),
        ),
        check_vma=False,
    )
```
